512 devices in a mesh: ctx: 64 (over x, z), head: 8 (over y, core).
Axes of the slice: x: 4, y: 4, z: 16, core: 2. Of those that a mesh axis runs over, the one named last changes fastest.
Arguments:
- inputs: bfloat16 [16384, 4096], P(('ctx', 'head')), may hold values from -0.3125 to 0.3125
- step_sizes: bfloat16 [16384, 64], P(('ctx', 'head')), may hold values from 0 to 16384, as said below
- decay_rates: float32 [64], P('head'), may hold values from 0 to 1, as said below
- state_write: bfloat16 [16384, 512], P(('ctx', 'head')), may hold values from -6 to 6
- state_read: bfloat16 [16384, 512], P(('ctx', 'head')), may hold values from -0.75 to 0.75
- doc_lengths: int32 [16], replicated, may hold values from 1 to 8192, 16384 in all
- out_grad: bfloat16 [16384, 4096], P(('ctx', 'head')), may hold values from -0.3125 to 0.3125
Outputs:
- outputs: bfloat16 [16384, 4096], P(('ctx', 'head'))
- input_grad: bfloat16 [16384, 4096], P(('ctx', 'head'))
- write_grad: bfloat16 [16384, 512], P(('ctx', 'head'))
- read_grad: bfloat16 [16384, 512], P(('ctx', 'head'))
The draws below stay inside these ranges and needn't reach their ends.
Inputs may be any that keep to these rules, and one draw needn't show every extreme that they name: `step_sizes`: positive steps; a few positions of the slab carry far larger steps than the others. `decay_rates`: positive rates. `doc_lengths`: the 16 lengths sum to 16384; the longest is exactly 8192.
All inputs are finite; a program needn't handle non-finite values.
Results may differ from the reference program's by a relative error of at most 0.012.
Values may be sent and summed in bfloat16 or wider, within the bound.
A program may use at most 128 MiB of HBM per device.

```python
import math
import jax
import jax.numpy as jnp
import numpy as np
from jax import lax

HEADS = 64
HEAD_DIM = 64
STATE = 64
GROUPS = 8
BLOCK = 256
DOCS = 16
TOKENS = 16384


def draw_step_sizes(key, part):
    base_key, place_key = jax.random.split(key)
    baseline = jax.random.uniform(base_key, (TOKENS, HEADS), jnp.float32, 0.5, 1.5)
    places = jax.random.randint(place_key, (3,), 0, TOKENS)
    matches = jnp.arange(TOKENS)[:, None] == places[None, :]
    bursting = jnp.any(matches, axis=1)
    return jnp.where(bursting[:, None], 0.7 * TOKENS, baseline).astype(jnp.bfloat16)


def draw_decay_rates(key, part):
    pick_key, slow_key, fast_key = jax.random.split(key, 3)
    share = 0.5
    chooser = jax.random.uniform(pick_key, (HEADS,), jnp.float32)
    slow_rate = jnp.exp(jax.random.uniform(slow_key, (HEADS,), jnp.float32, math.log(0.3), math.log(0.75))) / TOKENS
    fast_rate = jnp.exp(jax.random.uniform(fast_key, (HEADS,), jnp.float32, math.log(0.045), math.log(0.09)))
    return jnp.where(chooser < share, slow_rate, fast_rate)


def steps_of(own_key, extent, shards, smallest, high):
    loudness, own = 1.0, jax.random.fold_in(own_key, 6)
    for axis_at, parts in shards:
        draws = jnp.exp(jax.random.uniform(jax.random.fold_in(own, axis_at), (parts,), jnp.float32, smallest / len(shards), high / len(shards)))
        loudness = loudness * jnp.repeat(draws, extent[axis_at] // parts).reshape([-1 if axis == axis_at else 1 for axis in range(len(extent))])
    return loudness


def length_profile(amount, total, reach, slope):
    loads = [(1 << 20) // math.isqrt(grade ** slope) + 1 for grade in range(2, amount + 1)]
    spare, holding = total - reach - (amount - 1), [1] * (amount - 1)
    while spare > 0:
        candidates = [i for i in range(amount - 1) if holding[i] < reach]
        pool, budget = sum([loads[i] for i in candidates]), spare
        for i in candidates:
            addition = min(reach - holding[i], max(1, budget * loads[i] // pool), spare)
            holding[i] = holding[i] + addition
            spare = spare - addition
    return np.array([reach] + holding)


def uneven_parts(stream_key, amount, total, most, lean):
    if amount == 2:
        one = jax.random.randint(stream_key, (), max(1, total - most), min(most, total - 1) + 1)
        return jnp.stack([one, total - one])
    lengths = jnp.asarray(length_profile(amount, total, most, lean), jnp.int32)
    couples = (amount - 1) // 2
    donor, sink = lengths[1:1 + 2 * couples:2], lengths[2:2 + 2 * couples:2]
    slack = jnp.minimum(donor - 1, most - sink)
    moved = jax.random.randint(jax.random.fold_in(stream_key, 1), (couples,), 0, 1 << 20) % (slack + 1)
    lengths = lengths.at[1:1 + 2 * couples:2].set(donor - moved).at[2:2 + 2 * couples:2].set(sink + moved)
    return lengths[jax.random.permutation(jax.random.fold_in(stream_key, 2), amount)]


def noise(own_key, shape, width, most, shards=(), held_as=jnp.bfloat16):
    entries = jax.random.normal(own_key, shape, jnp.float32) * width
    if len(shards) > 0:
        entries = steps_of(own_key, shape, shards, -0.22, 0.18) * entries
    return jnp.clip(entries, min=-most, max=most).astype(held_as)


def setup_inputs(seed: int = 0) -> dict:
    streams_of = jax.random.split(jax.random.key(seed), 8)
    inputs = noise(streams_of[0], (TOKENS, HEADS * HEAD_DIM), 0.05, 0.3125, ((0, 512),))
    step_sizes = draw_step_sizes(jax.random.fold_in(streams_of[7], 71), 0)
    decay_rates = draw_decay_rates(jax.random.fold_in(streams_of[7], 71), 0)
    state_write = noise(streams_of[3], (TOKENS, GROUPS * STATE), 1.0, 6.0, ((0, 512),))
    state_read = noise(streams_of[4], (TOKENS, GROUPS * STATE), STATE ** -0.5, 0.75, ((0, 512),))
    doc_lengths = uneven_parts(streams_of[5], DOCS, TOKENS, TOKENS // 2, 2).astype(jnp.int32)
    out_grad = noise(streams_of[6], (TOKENS, HEADS * HEAD_DIM), 0.05, 0.3125, ((0, 512),))
    return {"inputs": inputs, "step_sizes": step_sizes, "decay_rates": decay_rates, "state_write": state_write, "state_read": state_read, "doc_lengths": doc_lengths, "out_grad": out_grad}


def segment_ids(doc_lengths, positions):
    ends = jnp.cumsum(doc_lengths)
    starts = ends - doc_lengths
    hits = (starts[None, :] <= positions[:, None]).astype(jnp.int32)
    return lax.optimization_barrier(jnp.sum(hits, axis=1)) - 1

def block_outputs(values, writers, readers, running, segment):
    scores = jnp.einsum('ign,jgn->gij', readers, writers, preferred_element_type=jnp.float32)
    levels = jnp.transpose(running, (1, 2, 0))
    spread = levels[:, :, :, None] - levels[:, :, None, :]
    length = segment.shape[0]
    row_index = lax.broadcasted_iota(jnp.int32, (length, length), 0)
    col_index = lax.broadcasted_iota(jnp.int32, (length, length), 1)
    allowed = (row_index >= col_index) & (segment[:, None] == segment[None, :])
    factor = jnp.where(allowed, jnp.exp(jnp.where(allowed, spread, 0.0)), 0.0)
    weights = (scores[:, None] * factor).astype(jnp.bfloat16)
    return jnp.einsum('ghij,jghp->ighp', weights, values, preferred_element_type=jnp.float32)

def carried_outputs(readers, running, segment, previous, carried):
    factor = jnp.where((segment == previous)[:, None, None], jnp.exp(running), 0.0)
    product = jnp.einsum('ign,ghnp->ighp', readers.astype(jnp.float32), carried, precision=lax.Precision.HIGHEST)
    return product * factor[..., None]

def block_state(values, writers, running, segment):
    final_sum = running[-1]
    allowed = segment == segment[-1]
    factor = jnp.where(allowed[:, None, None], jnp.exp(final_sum[None] - running), 0.0)
    weighted = (writers[:, :, None, :] * factor[..., None]).astype(jnp.bfloat16)
    return jnp.einsum('jghn,jghp->ghnp', weighted, values, preferred_element_type=jnp.float32)

def block_decay(running, segment, previous):
    return jnp.where(segment[-1] == previous, jnp.exp(running[-1]), 0.0)

def reference(inputs, step_sizes, decay_rates, state_write, state_read, doc_lengths, out_grad):
    blocks = TOKENS // BLOCK
    per_group = HEADS // GROUPS
    positions = jnp.arange(TOKENS, dtype=jnp.int32)
    segment = segment_ids(doc_lengths, positions).reshape(blocks, BLOCK)
    previous = segment_ids(doc_lengths, positions - 1).reshape(blocks, BLOCK)[:, 0]
    log_decay = -step_sizes.astype(jnp.float32) * decay_rates[None, :]
    running = jnp.cumsum(log_decay.reshape(blocks, BLOCK, GROUPS, per_group), axis=1)

    def advance(carried, pieces):
        piece_values, piece_writers, piece_readers, piece_running, piece_segment, piece_previous = pieces
        result = block_outputs(piece_values, piece_writers, piece_readers, piece_running, piece_segment)
        result = result + carried_outputs(piece_readers, piece_running, piece_segment, piece_previous, carried)
        decays = block_decay(piece_running, piece_segment, piece_previous)
        carried = decays[..., None, None] * carried + block_state(piece_values, piece_writers, piece_running, piece_segment)
        return (carried, result.astype(jnp.bfloat16))

    def forward(values, writers, readers):
        values = values.reshape(blocks, BLOCK, GROUPS, per_group, HEAD_DIM)
        writers = writers.reshape(blocks, BLOCK, GROUPS, STATE)
        readers = readers.reshape(blocks, BLOCK, GROUPS, STATE)
        initial = jnp.zeros((GROUPS, per_group, STATE, HEAD_DIM), jnp.float32)
        _, produced = lax.scan(jax.checkpoint(advance), initial, (values, writers, readers, running, segment, previous))
        return produced.reshape(TOKENS, HEADS * HEAD_DIM)
    outputs, pullback = jax.vjp(forward, inputs, state_write, state_read)
    input_grad, write_grad, read_grad = pullback(out_grad)
    return (outputs, input_grad, write_grad.reshape(TOKENS, GROUPS * STATE), read_grad.reshape(TOKENS, GROUPS * STATE))
```

```python
import functools

import jax
import jax.numpy as jnp
from jax import lax
from jax.experimental import pallas as pl
from jax.experimental.pallas import tpu as pltpu
from jax.sharding import PartitionSpec as P

HEAD_DIM = 64
STATE = 64
BLOCK = 256
DOCS = 16
HEADS_HERE = 8
WIDE = HEADS_HERE * HEAD_DIM
PAIRS = HEADS_HERE // 2
LANES = 128
NEG = -1e30
F32 = jnp.float32
BF16 = jnp.bfloat16


def dot_nn(a, b):
    return lax.dot_general(a, b, (((1,), (0,)), ((), ())), preferred_element_type=F32)


def dot_nt(a, b):
    return lax.dot_general(a, b, (((1,), (1,)), ((), ())), preferred_element_type=F32)


def dot_tn(a, b):
    return lax.dot_general(a, b, (((0,), (0,)), ((), ())), preferred_element_type=F32)


def kernel(
    nx, nz, ny,
    x_ref, step_ref, rate_ref, w_ref, r_ref, doc_ref, g_ref,
    out_ref, dx_ref, dw_ref, dr_ref,
    st_send, st_buf, wr_send, wr_buf, v_buf, g_buf,
    dec_send, dec_recv, f_send, f_recv, b_send, b_recv,
    xf_send, xf_recv, xb_send, xb_recv,
    rf_send, rf_recv, rb_send, rb_recv,
    out_send, dx_send, gw_send, gw_recv,
    run_col, run_row, bias_ref, score_ref, dscore_ref, ev_ref, cg_ref, loc_ref, dv_ref,
    y_ssem, y_rsem, z_ssem, z_rsem, x_ssem, x_rsem, own_sem,
):
    rows = BLOCK // ny
    blocks_of = nz // PAIRS
    piece = STATE // blocks_of
    ctx = lax.axis_index("ctx")
    me = lax.axis_index("head")
    zme = lax.rem(ctx, nz)
    xme = lax.div(ctx, nz)
    base = xme * nz

    def y_peer(k):
        return lax.rem(me + k, ny)

    def y_from(k):
        return lax.rem(me + ny - k, ny)

    def z_peer(k):
        return lax.rem(zme + k, nz)

    def z_from(k):
        return lax.rem(zme + nz - k, nz)

    def x_peer(k):
        return lax.rem(xme + k, nx)

    def x_from(k):
        return lax.rem(xme + nx - k, nx)

    def y_copy(cat, k, src, dst):
        return pltpu.make_async_remote_copy(
            src_ref=src, dst_ref=dst, send_sem=y_ssem.at[cat, k], recv_sem=y_rsem.at[cat, k],
            device_id={"ctx": ctx, "head": y_peer(k)}, device_id_type=pl.DeviceIdType.MESH)

    def z_copy(cat, k, src, dst):
        return pltpu.make_async_remote_copy(
            src_ref=src, dst_ref=dst, send_sem=z_ssem.at[cat, k], recv_sem=z_rsem.at[cat, k],
            device_id={"ctx": base + z_peer(k), "head": me}, device_id_type=pl.DeviceIdType.MESH)

    def x_copy(cat, k, src, dst):
        return pltpu.make_async_remote_copy(
            src_ref=src, dst_ref=dst, send_sem=x_ssem.at[cat, k], recv_sem=x_rsem.at[cat, k],
            device_id={"ctx": x_peer(k) * nz + zme, "head": me}, device_id_type=pl.DeviceIdType.MESH)

    def wide(at):
        return pl.ds(pl.multiple_of(at * WIDE, WIDE), WIDE)

    def z_offset(i):
        half = lax.div(i + 1, 2)
        return nz // 2 + half * (1 - 2 * lax.rem(i, 2))

    def each(count, body):
        def step(i, carry):
            body(i)
            return carry

        lax.fori_loop(0, count, step, 0)

    barrier = pltpu.get_barrier_semaphore()
    each(ny - 1, lambda i: pl.semaphore_signal(
        barrier, inc=1, device_id={"ctx": ctx, "head": y_peer(i + 1)}, device_id_type=pl.DeviceIdType.MESH))
    each(nx - 1, lambda i: pl.semaphore_signal(
        barrier, inc=1, device_id={"ctx": x_peer(i + 1) * nz + zme, "head": me}, device_id_type=pl.DeviceIdType.MESH))
    each(nz - 1, lambda i: pl.semaphore_signal(
        barrier, inc=1, device_id={"ctx": base + z_peer(i + 1), "head": me}, device_id_type=pl.DeviceIdType.MESH))

    own_v = pltpu.make_async_copy(x_ref.at[:, wide(me)], v_buf.at[me], own_sem.at[0])
    own_g = pltpu.make_async_copy(g_ref.at[:, wide(me)], g_buf.at[me], own_sem.at[1])
    own_v.start()
    own_g.start()
    low = lax.broadcasted_iota(jnp.int32, (rows, LANES), 1) < 64
    st_send[...] = jnp.zeros((rows, LANES), BF16)
    st_send[:, 0:ny * HEADS_HERE] = step_ref[...]
    for pair in range(ny // 2):
        cols = slice(pair * LANES, (pair + 1) * LANES)
        w2 = w_ref[:, cols].astype(F32)
        r2 = r_ref[:, cols].astype(F32)
        wr_send[2 * pair] = jnp.where(low, w2, pltpu.roll(r2, 64, 1)).astype(BF16)
        wr_send[2 * pair + 1] = jnp.where(low, pltpu.roll(w2, 64, 1), r2).astype(BF16)
    st_buf[me] = st_send[...]
    wr_buf[me] = wr_send[me]

    first = ctx * BLOCK
    starts, at = [], jnp.int32(0)
    for k in range(DOCS):
        starts.append(at)
        at = at + doc_ref[k]

    def segment(pos):
        seg = jnp.where(starts[0] <= pos, 1, 0)
        for k in range(1, DOCS):
            seg = seg + jnp.where(starts[k] <= pos, 1, 0)
        return seg

    seg_before = segment(first - 1)
    seg_last = segment(first + BLOCK - 1)
    seg_col = segment(first + lax.broadcasted_iota(jnp.int32, (BLOCK, LANES), 0))
    seg_row = segment(first + lax.broadcasted_iota(jnp.int32, (8, BLOCK), 1))[0:1]
    row_i = lax.broadcasted_iota(jnp.int32, (BLOCK, BLOCK), 0)
    col_i = lax.broadcasted_iota(jnp.int32, (BLOCK, BLOCK), 1)
    causal = row_i >= col_i
    seg_wide = jnp.concatenate([seg_col, seg_col], axis=1)
    bias_ref[...] = jnp.where(causal & (seg_wide == seg_row), 0.0, NEG)
    through = jnp.where(seg_last == seg_before, 1.0, 0.0)
    pl.semaphore_wait(barrier, ny - 1 + nz - 1 + nx - 1)

    def send_small(i):
        y_copy(0, i + 1, st_send, st_buf.at[me]).start()
        y_copy(1, i + 1, wr_send.at[y_peer(i + 1)], wr_buf.at[me]).start()

    each(ny - 1, send_small)
    each(ny - 1, lambda i: y_copy(2, i + 1, x_ref.at[:, wide(y_peer(i + 1))], v_buf.at[me]).start())
    each(ny - 1, lambda i: y_copy(3, i + 1, g_ref.at[:, wide(y_peer(i + 1))], g_buf.at[me]).start())

    each(ny - 1, lambda i: y_copy(0, i + 1, st_send, st_buf.at[y_from(i + 1)]).wait_recv())
    steps = st_buf[...].reshape(BLOCK, LANES)
    pick = (lax.broadcasted_iota(jnp.int32, (LANES, HEADS_HERE * LANES), 0) == me * HEADS_HERE
            + lax.broadcasted_iota(jnp.int32, (LANES, HEADS_HERE * LANES), 1) // LANES)
    spread_steps = dot_nn(steps, jnp.where(pick, 1.0, 0.0).astype(BF16)).astype(BF16)
    summed = dot_nn(jnp.where(causal, 1.0, 0.0).astype(BF16), spread_steps)
    pick_row = (lax.broadcasted_iota(jnp.int32, (16, LANES), 1) == me * HEADS_HERE
                + lax.broadcasted_iota(jnp.int32, (16, LANES), 0))
    steps_row = dot_nt(jnp.where(pick_row, 1.0, 0.0).astype(BF16), steps).astype(BF16)
    summed_row = dot_nn(steps_row, jnp.where(row_i <= col_i, 1.0, 0.0).astype(BF16))
    for h in range(HEADS_HERE):
        run_col[:, h * LANES:(h + 1) * LANES] = summed[:, h * LANES:(h + 1) * LANES] * (-rate_ref[h])
        run_row[h:h + 1, :] = summed_row[h:h + 1, :] * (-rate_ref[h])
    low = lax.broadcasted_iota(jnp.int32, (BLOCK, LANES), 1) < 64
    low_row = low[0:1]

    def pair_run(t):
        return jnp.where(low, run_col[:, 2 * t * LANES:(2 * t + 1) * LANES],
                         run_col[:, (2 * t + 1) * LANES:(2 * t + 2) * LANES])

    def pair_last(t):
        return jnp.where(low_row, run_col[BLOCK - 1:BLOCK, 2 * t * LANES:(2 * t + 1) * LANES],
                         run_col[BLOCK - 1:BLOCK, (2 * t + 1) * LANES:(2 * t + 2) * LANES])

    def factor_in(t):
        return jnp.where(seg_col == seg_before, jnp.exp(pair_run(t)), 0.0)

    def factor_out(t):
        return jnp.where(seg_col == seg_last, jnp.exp(pair_last(t) - pair_run(t)), 0.0)

    for t in range(PAIRS):
        dec_send[t] = jnp.exp(pair_last(t)) * through
    dec_recv[zme] = dec_send[zme // blocks_of]

    def send_decay(i):
        k = z_offset(i)
        z_copy(0, k, dec_send.at[lax.div(z_peer(k), blocks_of)], dec_recv.at[zme]).start()

    each(nz - 1, send_decay)

    each(ny - 1, lambda i: y_copy(1, i + 1, wr_send.at[y_peer(i + 1)], wr_buf.at[y_from(i + 1)]).wait_recv())
    wr = wr_buf[...].reshape(BLOCK, LANES)
    rw = pltpu.roll(wr.astype(F32), 64, 1)
    writers = wr[:, 0:64]
    readers = rw[:, 0:64].astype(BF16)
    read_low = jnp.where(low, rw, 0.0).astype(BF16)
    write_high = jnp.where(low, 0.0, rw).astype(BF16)
    score_ref[...] = dot_nt(readers, writers)

    own_v.wait()
    each(ny - 1, lambda i: y_copy(2, i + 1, x_ref.at[:, wide(y_peer(i + 1))], v_buf.at[y_from(i + 1)]).wait_recv())
    for t in range(PAIRS):
        cols = slice(t * LANES, (t + 1) * LANES)
        values = v_buf[:, :, cols].reshape(BLOCK, LANES)
        ev = (values.astype(F32) * factor_out(t)).astype(BF16)
        ev_ref[:, cols] = ev
        added = dot_tn(wr, ev)[0:STATE].astype(BF16)
        f_send[t * blocks_of:(t + 1) * blocks_of] = added.reshape(blocks_of, piece, LANES)

    def send_f(i):
        k = z_offset(i)
        z_copy(1, k, f_send.at[z_peer(k)], f_recv.at[zme]).start()

    each(nz - 1, send_f)
    f_recv[zme] = f_send[zme]

    own_g.wait()
    each(ny - 1, lambda i: y_copy(3, i + 1, g_ref.at[:, wide(y_peer(i + 1))], g_buf.at[y_from(i + 1)]).wait_recv())
    for t in range(PAIRS):
        cols = slice(t * LANES, (t + 1) * LANES)
        grads = g_buf[:, :, cols].reshape(BLOCK, LANES)
        cg = (grads.astype(F32) * factor_in(t)).astype(BF16)
        cg_ref[:, cols] = cg
        added = dot_tn(wr, cg)[STATE:2 * STATE].astype(BF16)
        b_send[t * blocks_of:(t + 1) * blocks_of] = added.reshape(blocks_of, piece, LANES)

    def send_b(i):
        k = z_offset(i)
        z_copy(2, k, b_send.at[z_peer(k)], b_recv.at[zme]).start()

    each(nz - 1, send_b)
    b_recv[zme] = b_send[zme]

    dscore_ref[...] = jnp.zeros((BLOCK, BLOCK), F32)
    low_one = jnp.where(low_row, 1.0, 0.0).astype(BF16)
    high_one = jnp.where(low_row, 0.0, 1.0).astype(BF16)

    def inside(t, carry):
        cols = pl.ds(pl.multiple_of(t * LANES, LANES), LANES)
        values = v_buf[:, :, cols].reshape(BLOCK, LANES)
        grads = g_buf[:, :, cols].reshape(BLOCK, LANES)
        local = jnp.zeros((BLOCK, LANES), F32)
        dvalue = jnp.zeros((BLOCK, LANES), F32)
        for half, ones in ((0, low_one), (1, high_one)):
            h = 2 * t + half
            column = run_col[:, pl.ds(pl.multiple_of(h * LANES, LANES), LANES)]
            row = run_row[pl.ds(h, 1), :]
            factor = jnp.exp(jnp.concatenate([column, column], axis=1) - row + bias_ref[...])
            weights = (score_ref[...] * factor).astype(BF16)
            half_grads = grads * ones
            local = local + dot_nn(weights, values * ones)
            dscore_ref[...] += dot_nt(half_grads, values) * factor
            dvalue = dvalue + dot_tn(weights, half_grads)
        loc_ref[:, cols] = local
        dv_ref[:, cols] = dvalue
        return carry

    lax.fori_loop(0, 2, inside, 0)

    each(nz - 1, lambda i: z_copy(0, i + 1, dec_send.at[0], dec_recv.at[z_from(i + 1)]).wait_recv())
    each(nz - 1, lambda i: z_copy(1, i + 1, f_send.at[0], f_recv.at[z_from(i + 1)]).wait_recv())
    total = jnp.zeros((piece, LANES), F32)
    product = jnp.ones((1, LANES), F32)
    for z in range(nz):
        total = dec_recv[z] * total + f_recv[z].astype(F32)
        product = dec_recv[z] * product
    xf_send[0:piece] = total
    xf_send[piece:piece + 8] = jnp.broadcast_to(product, (8, LANES))
    each(nx - 1, lambda i: x_copy(0, i + 1, xf_send, xf_recv.at[xme]).start())
    xf_recv[xme] = xf_send[...]
    each(nz - 1, lambda i: z_copy(2, i + 1, b_send.at[0], b_recv.at[z_from(i + 1)]).wait_recv())
    total = jnp.zeros((piece, LANES), F32)
    for z in reversed(range(nz)):
        total = dec_recv[z] * total + b_recv[z].astype(F32)
    xb_send[...] = total
    each(nx - 1, lambda i: x_copy(1, i + 1, xb_send, xb_recv.at[xme]).start())
    xb_recv[xme] = xb_send[...]

    lax.fori_loop(2, 3, inside, 0)

    each(nx - 1, lambda i: x_copy(0, i + 1, xf_send, xf_recv.at[x_from(i + 1)]).wait_recv())
    state = jnp.zeros((piece, LANES), F32)
    for x in range(nx):
        longer = xf_recv[x, piece:piece + 1] * state + xf_recv[x, 0:piece]
        state = jnp.where(x < xme, longer, state)
    for z in range(nz):
        rf_send[z] = state.astype(BF16)
        state = dec_recv[z] * state + f_recv[z].astype(F32)

    def return_f(i):
        k = z_offset(i)
        z_copy(3, k, rf_send.at[z_peer(k)], rf_recv.at[zme]).start()

    each(nz - 1, return_f)
    rf_recv[zme] = rf_send[zme]

    each(nx - 1, lambda i: x_copy(1, i + 1, xb_send, xb_recv.at[x_from(i + 1)]).wait_recv())
    state = jnp.zeros((piece, LANES), F32)
    for x in reversed(range(nx)):
        longer = xf_recv[x, piece:piece + 1] * state + xb_recv[x]
        state = jnp.where(x > xme, longer, state)
    for z in reversed(range(nz)):
        rb_send[z] = state.astype(BF16)
        state = dec_recv[z] * state + b_recv[z].astype(F32)

    def return_b(i):
        k = z_offset(i)
        z_copy(4, k, rb_send.at[z_peer(k)], rb_recv.at[zme]).start()

    each(nz - 1, return_b)
    rb_recv[zme] = rb_send[zme]

    lax.fori_loop(3, 4, inside, 0)
    dscore = dscore_ref[...].astype(BF16)
    gw = dot_nn(dscore, write_high) + dot_tn(dscore, read_low)
    nothing = jnp.zeros((STATE, LANES), BF16)

    each(nz - 1, lambda i: z_copy(3, i + 1, rf_send.at[0], rf_recv.at[z_from(i + 1)]).wait_recv())
    for t in range(PAIRS):
        cols = slice(t * LANES, (t + 1) * LANES)
        entering = rf_recv[t * blocks_of:(t + 1) * blocks_of].reshape(STATE, LANES)
        result = loc_ref[:, cols] + factor_in(t) * dot_nn(readers, entering)
        out_send[:, :, cols] = result.astype(BF16).reshape(ny, rows, LANES)
        gw = gw + dot_nt(cg_ref[:, cols], jnp.concatenate([nothing, entering], axis=0))
    each(ny - 1, lambda i: y_copy(4, i + 1, out_send.at[y_peer(i + 1)], out_ref.at[:, wide(me)]).start())
    own_out = pltpu.make_async_copy(out_send.at[me], out_ref.at[:, wide(me)], own_sem.at[2])
    own_out.start()

    each(nz - 1, lambda i: z_copy(4, i + 1, rb_send.at[0], rb_recv.at[z_from(i + 1)]).wait_recv())
    for t in range(PAIRS):
        cols = slice(t * LANES, (t + 1) * LANES)
        leaving = rb_recv[t * blocks_of:(t + 1) * blocks_of].reshape(STATE, LANES)
        result = dv_ref[:, cols] + factor_out(t) * dot_nn(writers, leaving)
        dx_send[:, :, cols] = result.astype(BF16).reshape(ny, rows, LANES)
        gw = gw + dot_nt(ev_ref[:, cols], jnp.concatenate([leaving, nothing], axis=0))
    gw_send[...] = gw.astype(BF16).reshape(ny, rows, LANES)
    each(ny - 1, lambda i: y_copy(6, i + 1, gw_send.at[y_peer(i + 1)], gw_recv.at[me]).start())
    each(ny - 1, lambda i: y_copy(5, i + 1, dx_send.at[y_peer(i + 1)], dx_ref.at[:, wide(me)]).start())
    own_dx = pltpu.make_async_copy(dx_send.at[me], dx_ref.at[:, wide(me)], own_sem.at[3])
    own_dx.start()
    gw_recv[me] = gw_send[me]

    def drain_y(i):
        k = i + 1
        y_copy(0, k, st_send, st_buf.at[me]).wait_send()
        y_copy(1, k, wr_send.at[y_peer(k)], wr_buf.at[me]).wait_send()
        y_copy(2, k, x_ref.at[:, wide(y_peer(k))], v_buf.at[me]).wait_send()
        y_copy(3, k, g_ref.at[:, wide(y_peer(k))], g_buf.at[me]).wait_send()

    def drain_z(i):
        k = i + 1
        z_copy(0, k, dec_send.at[0], dec_recv.at[zme]).wait_send()
        z_copy(1, k, f_send.at[z_peer(k)], f_recv.at[zme]).wait_send()
        z_copy(2, k, b_send.at[z_peer(k)], b_recv.at[zme]).wait_send()
        z_copy(3, k, rf_send.at[z_peer(k)], rf_recv.at[zme]).wait_send()
        z_copy(4, k, rb_send.at[z_peer(k)], rb_recv.at[zme]).wait_send()

    def drain_x(i):
        k = i + 1
        x_copy(0, k, xf_send, xf_recv.at[xme]).wait_send()
        x_copy(1, k, xb_send, xb_recv.at[xme]).wait_send()

    each(ny - 1, drain_y)
    each(nz - 1, drain_z)
    each(nx - 1, drain_x)

    each(ny - 1, lambda i: y_copy(6, i + 1, gw_send.at[y_peer(i + 1)], gw_recv.at[y_from(i + 1)]).wait_recv())
    low = lax.broadcasted_iota(jnp.int32, (rows, LANES), 1) < 64
    for pair in range(ny // 2):
        cols = slice(pair * LANES, (pair + 1) * LANES)
        even = gw_recv[2 * pair].astype(F32)
        odd = gw_recv[2 * pair + 1].astype(F32)
        dw_ref[:, cols] = jnp.where(low, even, pltpu.roll(odd, 64, 1)).astype(BF16)
        dr_ref[:, cols] = jnp.where(low, pltpu.roll(even, 64, 1), odd).astype(BF16)

    def finish(i):
        k = i + 1
        y_copy(4, k, out_send.at[y_peer(k)], out_ref.at[:, wide(y_from(k))]).wait()
        y_copy(5, k, dx_send.at[y_peer(k)], dx_ref.at[:, wide(y_from(k))]).wait()
        y_copy(6, k, gw_send.at[y_peer(k)], gw_recv.at[me]).wait_send()

    each(ny - 1, finish)
    own_out.wait()
    own_dx.wait()


def on_device(nx, nz, ny, inputs, step_sizes, decay_rates, state_write, state_read, doc_lengths, out_grad):
    rows = BLOCK // ny
    piece = STATE // (nz // PAIRS)
    vmem = pl.BlockSpec(memory_space=pltpu.VMEM)
    smem = pl.BlockSpec(memory_space=pltpu.SMEM)
    anywhere = pl.BlockSpec(memory_space=pl.ANY)
    wide_shape = jax.ShapeDtypeStruct(inputs.shape, BF16)
    thin_shape = jax.ShapeDtypeStruct(state_write.shape, BF16)
    bf = lambda *shape: pltpu.VMEM(shape, BF16)
    fl = lambda *shape: pltpu.VMEM(shape, F32)
    return pl.pallas_call(
        functools.partial(kernel, nx, nz, ny),
        out_shape=(wide_shape, wide_shape, thin_shape, thin_shape),
        in_specs=[anywhere, vmem, smem, vmem, vmem, smem, anywhere],
        out_specs=(anywhere, anywhere, vmem, vmem),
        scratch_shapes=[
            bf(rows, LANES), bf(ny, rows, LANES), bf(ny, rows, LANES), bf(ny, rows, LANES),
            bf(ny, rows, WIDE), bf(ny, rows, WIDE),
            fl(PAIRS, 1, LANES), fl(nz, 1, LANES),
            bf(nz, piece, LANES), bf(nz, piece, LANES), bf(nz, piece, LANES), bf(nz, piece, LANES),
            fl(piece + 8, LANES), fl(nx, piece + 8, LANES), fl(piece, LANES), fl(nx, piece, LANES),
            bf(nz, piece, LANES), bf(nz, piece, LANES), bf(nz, piece, LANES), bf(nz, piece, LANES),
            bf(ny, rows, WIDE), bf(ny, rows, WIDE), bf(ny, rows, LANES), bf(ny, rows, LANES),
            fl(BLOCK, HEADS_HERE * LANES), fl(HEADS_HERE, BLOCK), fl(BLOCK, BLOCK), fl(BLOCK, BLOCK),
            fl(BLOCK, BLOCK), bf(BLOCK, WIDE), bf(BLOCK, WIDE), fl(BLOCK, WIDE), fl(BLOCK, WIDE),
            pltpu.SemaphoreType.DMA((7, ny)), pltpu.SemaphoreType.DMA((7, ny)),
            pltpu.SemaphoreType.DMA((5, nz)), pltpu.SemaphoreType.DMA((5, nz)),
            pltpu.SemaphoreType.DMA((2, nx)), pltpu.SemaphoreType.DMA((2, nx)),
            pltpu.SemaphoreType.DMA((4,)),
        ],
        compiler_params=pltpu.CompilerParams(collective_id=0, has_side_effects=True),
    )(inputs, step_sizes, decay_rates, state_write, state_read, doc_lengths, out_grad)


def solution(mesh):
    nctx, ny = mesh.shape["ctx"], mesh.shape["head"]
    nz = 16 if nctx % 16 == 0 else nctx // 2
    nx = nctx // nz
    rows = P(("ctx", "head"), None)
    return jax.shard_map(
        functools.partial(on_device, nx, nz, ny),
        mesh=mesh,
        in_specs=(rows, rows, P("head"), rows, rows, P(), rows),
        out_specs=(rows, rows, rows, rows),
        check_vma=False,
    )
```

```python
import functools

import jax
import jax.numpy as jnp
from jax import lax
from jax.experimental import pallas as pl
from jax.experimental.pallas import tpu as pltpu
from jax.sharding import PartitionSpec as P

HEAD_DIM = 64
STATE = 64
BLOCK = 256
DOCS = 16
HEADS_HERE = 8
WIDE = HEADS_HERE * HEAD_DIM
PAIRS = HEADS_HERE // 2
LANES = 128
NEG = -1e30
F32 = jnp.float32
BF16 = jnp.bfloat16


def dot_nn(a, b):
    return lax.dot_general(a, b, (((1,), (0,)), ((), ())), preferred_element_type=F32)


def dot_nt(a, b):
    return lax.dot_general(a, b, (((1,), (1,)), ((), ())), preferred_element_type=F32)


def dot_tn(a, b):
    return lax.dot_general(a, b, (((0,), (0,)), ((), ())), preferred_element_type=F32)


def kernel(
    nx, nz, ny,
    x_ref, step_ref, rate_ref, w_ref, r_ref, doc_ref, g_ref,
    out_ref, dx_ref, gw_recv,
    x_in, g_in, step_in, w_in, r_in, rate_in, doc_in,
    st_send, st_buf, wr_send, wr_buf, v_buf, g_buf,
    dec_send, dec_recv, f_send, f_recv, b_send, b_recv,
    xf_send, xf_recv, xb_send, xb_recv,
    rf_send, rf_recv, rb_send, rb_recv,
    out_send, dx_send, gw_send,
    run_col, run_row, bias_ref, score_ref, dscore_ref, ev_ref, cg_ref, loc_ref, dv_ref,
    y_ssem, y_rsem, z_ssem, z_rsem, x_ssem, x_rsem, own_sem, ready,
):
    rows = BLOCK // ny
    blocks_of = nz // PAIRS
    piece = STATE // blocks_of
    ctx = lax.axis_index("ctx")
    me = lax.axis_index("head")
    zme = lax.rem(ctx, nz)
    xme = lax.div(ctx, nz)
    base = xme * nz

    def y_peer(k):
        return lax.rem(me + k, ny)

    def y_from(k):
        return lax.rem(me + ny - k, ny)

    def z_peer(k):
        return lax.rem(zme + k, nz)

    def z_from(k):
        return lax.rem(zme + nz - k, nz)

    def x_peer(k):
        return lax.rem(xme + k, nx)

    def x_from(k):
        return lax.rem(xme + nx - k, nx)

    def y_copy(cat, k, src, dst):
        return pltpu.make_async_remote_copy(
            src_ref=src, dst_ref=dst, send_sem=y_ssem.at[cat, k], recv_sem=y_rsem.at[cat, k],
            device_id={"ctx": ctx, "head": y_peer(k)}, device_id_type=pl.DeviceIdType.MESH)

    def z_copy(cat, k, src, dst):
        return pltpu.make_async_remote_copy(
            src_ref=src, dst_ref=dst, send_sem=z_ssem.at[cat, k], recv_sem=z_rsem.at[cat, k],
            device_id={"ctx": base + z_peer(k), "head": me}, device_id_type=pl.DeviceIdType.MESH)

    def x_copy(cat, k, src, dst):
        return pltpu.make_async_remote_copy(
            src_ref=src, dst_ref=dst, send_sem=x_ssem.at[cat, k], recv_sem=x_rsem.at[cat, k],
            device_id={"ctx": x_peer(k) * nz + zme, "head": me}, device_id_type=pl.DeviceIdType.MESH)

    def signal_y(sem, k):
        pl.semaphore_signal(
            sem, inc=1, device_id={"ctx": ctx, "head": y_peer(k)}, device_id_type=pl.DeviceIdType.MESH)

    def signal_z(sem, k):
        pl.semaphore_signal(
            sem, inc=1, device_id={"ctx": base + z_peer(k), "head": me}, device_id_type=pl.DeviceIdType.MESH)

    def signal_x(sem, k):
        pl.semaphore_signal(
            sem, inc=1, device_id={"ctx": x_peer(k) * nz + zme, "head": me}, device_id_type=pl.DeviceIdType.MESH)

    def wide(at):
        return pl.ds(pl.multiple_of(at * WIDE, WIDE), WIDE)

    def z_offset(i):
        half = lax.div(i + 1, 2)
        return nz // 2 + half * (1 - 2 * lax.rem(i, 2))

    def each(count, body):
        def step(i, carry):
            body(i)
            return carry

        lax.fori_loop(0, count, step, 0)

    barrier = pltpu.get_barrier_semaphore()
    x_near = sorted({1, nx - 1})
    each(ny - 1, lambda i: signal_y(barrier, i + 1))
    for k in x_near:
        signal_x(barrier, k)
    for k in (1, nz - 1):
        signal_z(barrier, k)

    fetch = [
        pltpu.make_async_copy(src, dst, own_sem.at[i])
        for i, (src, dst) in enumerate((
            (step_ref, step_in), (w_ref, w_in), (r_ref, r_in), (x_ref, x_in), (g_ref, g_in),
            (doc_ref, doc_in), (rate_ref, rate_in)))
    ]
    for copy in fetch:
        copy.start()

    low = lax.broadcasted_iota(jnp.int32, (rows, LANES), 1) < 64
    st_send[...] = jnp.zeros((rows, LANES), BF16)
    for copy in fetch[0:3]:
        copy.wait()
    st_send[:, 0:ny * HEADS_HERE] = step_in[...]
    for pair in range(ny // 2):
        cols = slice(pair * LANES, (pair + 1) * LANES)
        w2 = w_in[:, cols].astype(F32)
        r2 = r_in[:, cols].astype(F32)
        wr_send[2 * pair] = jnp.where(low, w2, pltpu.roll(r2, 64, 1)).astype(BF16)
        wr_send[2 * pair + 1] = jnp.where(low, pltpu.roll(w2, 64, 1), r2).astype(BF16)
    fetch[3].wait()
    fetch[4].wait()
    pl.semaphore_wait(barrier, ny - 1 + len(x_near) + 2)

    def send_small(i):
        y_copy(0, i + 1, st_send, st_buf.at[me]).start()
        y_copy(1, i + 1, wr_send.at[y_peer(i + 1)], wr_buf.at[me]).start()

    each(ny - 1, send_small)
    each(ny - 1, lambda i: y_copy(2, i + 1, x_in.at[:, wide(y_peer(i + 1))], v_buf.at[me]).start())
    each(ny - 1, lambda i: y_copy(3, i + 1, g_in.at[:, wide(y_peer(i + 1))], g_buf.at[me]).start())

    steps_z = []
    radius = 1
    while radius < nz // 2:
        steps_z.append(radius)
        radius *= 2

    def reach_start(at):
        for k in (steps_z[at], nz - steps_z[at]):
            signal_z(ready.at[at], k)

    def reach_end(at):
        pl.semaphore_wait(ready.at[at], 2)

    reach_start(0)
    if nx > 2:
        signal_x(ready.at[3], 1)
        signal_x(ready.at[3], nx - 1)
    v_buf[me] = x_in[:, wide(me)]
    g_buf[me] = g_in[:, wide(me)]
    st_buf[me] = st_send[...]
    wr_buf[me] = wr_send[me]
    fetch[5].wait()
    fetch[6].wait()
    first = ctx * BLOCK
    starts, at = [], jnp.int32(0)
    for k in range(DOCS):
        starts.append(at)
        at = at + doc_in[k]

    def segment(pos):
        seg = jnp.where(starts[0] <= pos, 1, 0)
        for k in range(1, DOCS):
            seg = seg + jnp.where(starts[k] <= pos, 1, 0)
        return seg

    seg_before = segment(first - 1)
    seg_last = segment(first + BLOCK - 1)
    reach_end(0)
    if len(steps_z) > 1:
        reach_start(1)
    seg_col = segment(first + lax.broadcasted_iota(jnp.int32, (BLOCK, LANES), 0))
    seg_row = segment(first + lax.broadcasted_iota(jnp.int32, (8, BLOCK), 1))[0:1]
    row_i = lax.broadcasted_iota(jnp.int32, (BLOCK, BLOCK), 0)
    col_i = lax.broadcasted_iota(jnp.int32, (BLOCK, BLOCK), 1)
    causal = row_i >= col_i
    seg_wide = jnp.concatenate([seg_col, seg_col], axis=1)
    bias_ref[...] = jnp.where(causal & (seg_wide == seg_row), 0.0, NEG)
    dscore_ref[...] = jnp.zeros((BLOCK, BLOCK), F32)
    through = jnp.where(seg_last == seg_before, 1.0, 0.0)
    if nx > 2:
        pl.semaphore_wait(ready.at[3], 2)
    if len(steps_z) > 1:
        reach_end(1)
    if len(steps_z) > 2:
        reach_start(2)

    each(ny - 1, lambda i: y_copy(0, i + 1, st_send, st_buf.at[y_from(i + 1)]).wait_recv())
    steps = st_buf[...].reshape(BLOCK, LANES)
    pick = (lax.broadcasted_iota(jnp.int32, (LANES, HEADS_HERE * LANES), 0) == me * HEADS_HERE
            + lax.broadcasted_iota(jnp.int32, (LANES, HEADS_HERE * LANES), 1) // LANES)
    spread_steps = dot_nn(steps, jnp.where(pick, 1.0, 0.0).astype(BF16)).astype(BF16)
    summed = dot_nn(jnp.where(causal, 1.0, 0.0).astype(BF16), spread_steps)
    pick_row = (lax.broadcasted_iota(jnp.int32, (16, LANES), 1) == me * HEADS_HERE
                + lax.broadcasted_iota(jnp.int32, (16, LANES), 0))
    steps_row = dot_nt(jnp.where(pick_row, 1.0, 0.0).astype(BF16), steps).astype(BF16)
    summed_row = dot_nn(steps_row, jnp.where(row_i <= col_i, 1.0, 0.0).astype(BF16))
    for h in range(HEADS_HERE):
        run_col[:, h * LANES:(h + 1) * LANES] = summed[:, h * LANES:(h + 1) * LANES] * (-rate_in[h])
        run_row[h:h + 1, :] = summed_row[h:h + 1, :] * (-rate_in[h])
    low = lax.broadcasted_iota(jnp.int32, (BLOCK, LANES), 1) < 64
    low_row = low[0:1]

    def pair_run(t):
        return jnp.where(low, run_col[:, 2 * t * LANES:(2 * t + 1) * LANES],
                         run_col[:, (2 * t + 1) * LANES:(2 * t + 2) * LANES])

    def pair_last(t):
        return jnp.where(low_row, run_col[BLOCK - 1:BLOCK, 2 * t * LANES:(2 * t + 1) * LANES],
                         run_col[BLOCK - 1:BLOCK, (2 * t + 1) * LANES:(2 * t + 2) * LANES])

    def factor_in(t):
        return jnp.where(seg_col == seg_before, jnp.exp(pair_run(t)), 0.0)

    def factor_out(t):
        return jnp.where(seg_col == seg_last, jnp.exp(pair_last(t) - pair_run(t)), 0.0)

    for t in range(PAIRS):
        dec_send[t] = jnp.exp(pair_last(t)) * through
    dec_recv[zme] = dec_send[zme // blocks_of]

    def send_decay(i):
        k = z_offset(i)
        z_copy(0, k, dec_send.at[lax.div(z_peer(k), blocks_of)], dec_recv.at[zme]).start()

    if len(steps_z) > 2:
        reach_end(2)
    each(nz - 1, send_decay)

    each(ny - 1, lambda i: y_copy(1, i + 1, wr_send.at[y_peer(i + 1)], wr_buf.at[y_from(i + 1)]).wait_recv())
    wr = wr_buf[...].reshape(BLOCK, LANES)
    rw = pltpu.roll(wr.astype(F32), 64, 1)
    writers = wr[:, 0:64]
    readers = rw[:, 0:64].astype(BF16)
    read_low = jnp.where(low, rw, 0.0).astype(BF16)
    write_high = jnp.where(low, 0.0, rw).astype(BF16)
    score_ref[...] = dot_nt(readers, writers)

    each(ny - 1, lambda i: y_copy(2, i + 1, x_in.at[:, wide(y_peer(i + 1))], v_buf.at[y_from(i + 1)]).wait_recv())
    for t in range(PAIRS):
        cols = slice(t * LANES, (t + 1) * LANES)
        values = v_buf[:, :, cols].reshape(BLOCK, LANES)
        ev = (values.astype(F32) * factor_out(t)).astype(BF16)
        ev_ref[:, cols] = ev
        added = dot_tn(wr, ev)[0:STATE].astype(BF16)
        f_send[t * blocks_of:(t + 1) * blocks_of] = added.reshape(blocks_of, piece, LANES)

    def send_f(i):
        k = z_offset(i)
        z_copy(1, k, f_send.at[z_peer(k)], f_recv.at[zme]).start()

    each(nz - 1, send_f)
    f_recv[zme] = f_send[zme]

    each(ny - 1, lambda i: y_copy(3, i + 1, g_in.at[:, wide(y_peer(i + 1))], g_buf.at[y_from(i + 1)]).wait_recv())
    for t in range(PAIRS):
        cols = slice(t * LANES, (t + 1) * LANES)
        grads = g_buf[:, :, cols].reshape(BLOCK, LANES)
        cg = (grads.astype(F32) * factor_in(t)).astype(BF16)
        cg_ref[:, cols] = cg
        added = dot_tn(wr, cg)[STATE:2 * STATE].astype(BF16)
        b_send[t * blocks_of:(t + 1) * blocks_of] = added.reshape(blocks_of, piece, LANES)

    def send_b(i):
        k = z_offset(i)
        z_copy(2, k, b_send.at[z_peer(k)], b_recv.at[zme]).start()

    each(nz - 1, send_b)
    b_recv[zme] = b_send[zme]

    low_one = jnp.where(low_row, 1.0, 0.0).astype(BF16)
    high_one = jnp.where(low_row, 0.0, 1.0).astype(BF16)

    def inside(t, carry):
        cols = pl.ds(pl.multiple_of(t * LANES, LANES), LANES)
        values = v_buf[:, :, cols].reshape(BLOCK, LANES)
        grads = g_buf[:, :, cols].reshape(BLOCK, LANES)
        local = jnp.zeros((BLOCK, LANES), F32)
        dvalue = jnp.zeros((BLOCK, LANES), F32)
        for half, ones in ((0, low_one), (1, high_one)):
            h = 2 * t + half
            column = run_col[:, pl.ds(pl.multiple_of(h * LANES, LANES), LANES)]
            row = run_row[pl.ds(h, 1), :]
            factor = jnp.exp(jnp.concatenate([column, column], axis=1) - row + bias_ref[...])
            weights = (score_ref[...] * factor).astype(BF16)
            half_grads = grads * ones
            local = local + dot_nn(weights, values * ones)
            dscore_ref[...] += dot_nt(half_grads, values) * factor
            dvalue = dvalue + dot_tn(weights, half_grads)
        loc_ref[:, cols] = local
        dv_ref[:, cols] = dvalue
        return carry

    lax.fori_loop(0, 2, inside, 0)

    each(nz - 1, lambda i: z_copy(0, i + 1, dec_send.at[0], dec_recv.at[z_from(i + 1)]).wait_recv())
    each(nz - 1, lambda i: z_copy(1, i + 1, f_send.at[0], f_recv.at[z_from(i + 1)]).wait_recv())
    total = jnp.zeros((piece, LANES), F32)
    product = jnp.ones((1, LANES), F32)
    for z in range(nz):
        total = dec_recv[z] * total + f_recv[z].astype(F32)
        product = dec_recv[z] * product
    xf_send[0:piece] = total
    xf_send[piece:piece + 8] = jnp.broadcast_to(product, (8, LANES))
    each(nx - 1, lambda i: x_copy(0, i + 1, xf_send, xf_recv.at[xme]).start())
    xf_recv[xme] = xf_send[...]
    each(nz - 1, lambda i: z_copy(2, i + 1, b_send.at[0], b_recv.at[z_from(i + 1)]).wait_recv())
    total = jnp.zeros((piece, LANES), F32)
    for z in reversed(range(nz)):
        total = dec_recv[z] * total + b_recv[z].astype(F32)
    xb_send[...] = total
    each(nx - 1, lambda i: x_copy(1, i + 1, xb_send, xb_recv.at[xme]).start())
    xb_recv[xme] = xb_send[...]

    lax.fori_loop(2, 3, inside, 0)

    each(nx - 1, lambda i: x_copy(0, i + 1, xf_send, xf_recv.at[x_from(i + 1)]).wait_recv())
    state = jnp.zeros((piece, LANES), F32)
    for x in range(nx):
        longer = xf_recv[x, piece:piece + 1] * state + xf_recv[x, 0:piece]
        state = jnp.where(x < xme, longer, state)
    for z in range(nz):
        rf_send[z] = state.astype(BF16)
        state = dec_recv[z] * state + f_recv[z].astype(F32)

    def return_f(i):
        k = z_offset(i)
        z_copy(3, k, rf_send.at[z_peer(k)], rf_recv.at[zme]).start()

    each(nz - 1, return_f)
    rf_recv[zme] = rf_send[zme]

    each(nx - 1, lambda i: x_copy(1, i + 1, xb_send, xb_recv.at[x_from(i + 1)]).wait_recv())
    state = jnp.zeros((piece, LANES), F32)
    for x in reversed(range(nx)):
        longer = xf_recv[x, piece:piece + 1] * state + xb_recv[x]
        state = jnp.where(x > xme, longer, state)
    for z in reversed(range(nz)):
        rb_send[z] = state.astype(BF16)
        state = dec_recv[z] * state + b_recv[z].astype(F32)

    def return_b(i):
        k = z_offset(i)
        z_copy(4, k, rb_send.at[z_peer(k)], rb_recv.at[zme]).start()

    each(nz - 1, return_b)
    rb_recv[zme] = rb_send[zme]

    lax.fori_loop(3, 4, inside, 0)
    dscore = dscore_ref[...].astype(BF16)
    gw = dot_nn(dscore, write_high) + dot_tn(dscore, read_low)
    nothing = jnp.zeros((STATE, LANES), BF16)

    each(nz - 1, lambda i: z_copy(3, i + 1, rf_send.at[0], rf_recv.at[z_from(i + 1)]).wait_recv())
    for t in range(PAIRS):
        cols = slice(t * LANES, (t + 1) * LANES)
        entering = rf_recv[t * blocks_of:(t + 1) * blocks_of].reshape(STATE, LANES)
        result = loc_ref[:, cols] + factor_in(t) * dot_nn(readers, entering)
        out_send[:, :, cols] = result.astype(BF16).reshape(ny, rows, LANES)
        gw = gw + dot_nt(cg_ref[:, cols], jnp.concatenate([nothing, entering], axis=0))
    each(ny - 1, lambda i: y_copy(4, i + 1, out_send.at[y_peer(i + 1)], out_ref.at[:, wide(me)]).start())
    out_ref[:, wide(me)] = out_send[me]

    each(nz - 1, lambda i: z_copy(4, i + 1, rb_send.at[0], rb_recv.at[z_from(i + 1)]).wait_recv())
    for t in range(PAIRS):
        cols = slice(t * LANES, (t + 1) * LANES)
        leaving = rb_recv[t * blocks_of:(t + 1) * blocks_of].reshape(STATE, LANES)
        result = dv_ref[:, cols] + factor_out(t) * dot_nn(writers, leaving)
        dx_send[:, :, cols] = result.astype(BF16).reshape(ny, rows, LANES)
        gw = gw + dot_nt(ev_ref[:, cols], jnp.concatenate([leaving, nothing], axis=0))
    gw_send[...] = gw.astype(BF16).reshape(ny, rows, LANES)
    each(ny - 1, lambda i: y_copy(6, i + 1, gw_send.at[y_peer(i + 1)], gw_recv.at[me]).start())
    each(ny - 1, lambda i: y_copy(5, i + 1, dx_send.at[y_peer(i + 1)], dx_ref.at[:, wide(me)]).start())
    dx_ref[:, wide(me)] = dx_send[me]
    gw_recv[me] = gw_send[me]

    def drain_y(i):
        k = i + 1
        y_copy(0, k, st_send, st_buf.at[me]).wait_send()
        y_copy(1, k, wr_send.at[y_peer(k)], wr_buf.at[me]).wait_send()
        y_copy(2, k, x_in.at[:, wide(y_peer(k))], v_buf.at[me]).wait_send()
        y_copy(3, k, g_in.at[:, wide(y_peer(k))], g_buf.at[me]).wait_send()

    def drain_z(i):
        k = i + 1
        z_copy(0, k, dec_send.at[0], dec_recv.at[zme]).wait_send()
        z_copy(1, k, f_send.at[z_peer(k)], f_recv.at[zme]).wait_send()
        z_copy(2, k, b_send.at[z_peer(k)], b_recv.at[zme]).wait_send()
        z_copy(3, k, rf_send.at[z_peer(k)], rf_recv.at[zme]).wait_send()
        z_copy(4, k, rb_send.at[z_peer(k)], rb_recv.at[zme]).wait_send()

    def drain_x(i):
        k = i + 1
        x_copy(0, k, xf_send, xf_recv.at[xme]).wait_send()
        x_copy(1, k, xb_send, xb_recv.at[xme]).wait_send()

    each(ny - 1, drain_y)
    each(nz - 1, drain_z)
    each(nx - 1, drain_x)

    def finish(i):
        k = i + 1
        y_copy(4, k, out_send.at[y_peer(k)], out_ref.at[:, wide(y_from(k))]).wait()
        y_copy(6, k, gw_send.at[y_peer(k)], gw_recv.at[y_from(k)]).wait()
        y_copy(5, k, dx_send.at[y_peer(k)], dx_ref.at[:, wide(y_from(k))]).wait()

    each(ny - 1, finish)


def last(ny, out_in, dx_in, gw_in, out_ref, dx_ref, dw_ref, dr_ref, dw_out, dr_out, sem):
    rows = BLOCK // ny
    out_copy = pltpu.make_async_copy(out_in, out_ref, sem.at[0])
    dx_copy = pltpu.make_async_copy(dx_in, dx_ref, sem.at[1])
    dw_copy = pltpu.make_async_copy(dw_out, dw_ref, sem.at[2])
    dr_copy = pltpu.make_async_copy(dr_out, dr_ref, sem.at[3])
    out_copy.start()
    dx_copy.start()
    low = lax.broadcasted_iota(jnp.int32, (rows, LANES), 1) < 64
    for pair in range(ny // 2):
        cols = slice(pair * LANES, (pair + 1) * LANES)
        even = gw_in[2 * pair].astype(F32)
        odd = gw_in[2 * pair + 1].astype(F32)
        dw_out[:, cols] = jnp.where(low, even, pltpu.roll(odd, 64, 1)).astype(BF16)
        dr_out[:, cols] = jnp.where(low, pltpu.roll(even, 64, 1), odd).astype(BF16)
    dw_copy.start()
    dr_copy.start()
    out_copy.wait()
    dx_copy.wait()
    dw_copy.wait()
    dr_copy.wait()


def on_device(nx, nz, ny, inputs, step_sizes, decay_rates, state_write, state_read, doc_lengths, out_grad):
    rows = BLOCK // ny
    piece = STATE // (nz // PAIRS)
    vmem = pl.BlockSpec(memory_space=pltpu.VMEM)
    anywhere = pl.BlockSpec(memory_space=pl.ANY)
    wide_shape = jax.ShapeDtypeStruct(inputs.shape, BF16)
    thin_shape = jax.ShapeDtypeStruct(state_write.shape, BF16)
    bf = lambda *shape: pltpu.VMEM(shape, BF16)
    fl = lambda *shape: pltpu.VMEM(shape, F32)
    outs = pl.pallas_call(
        functools.partial(kernel, nx, nz, ny),
        out_shape=(bf(*inputs.shape), bf(*inputs.shape), bf(ny, rows, LANES)),
        in_specs=[anywhere] * 7,
        out_specs=(vmem, vmem, vmem),
        scratch_shapes=[
            bf(rows, ny * WIDE), bf(rows, ny * WIDE), bf(*step_sizes.shape), bf(*state_write.shape),
            bf(*state_read.shape), pltpu.SMEM(decay_rates.shape, F32), pltpu.SMEM((DOCS,), jnp.int32),
            bf(rows, LANES), bf(ny, rows, LANES), bf(ny, rows, LANES), bf(ny, rows, LANES),
            bf(ny, rows, WIDE), bf(ny, rows, WIDE),
            fl(PAIRS, 1, LANES), fl(nz, 1, LANES),
            bf(nz, piece, LANES), bf(nz, piece, LANES), bf(nz, piece, LANES), bf(nz, piece, LANES),
            fl(piece + 8, LANES), fl(nx, piece + 8, LANES), fl(piece, LANES), fl(nx, piece, LANES),
            bf(nz, piece, LANES), bf(nz, piece, LANES), bf(nz, piece, LANES), bf(nz, piece, LANES),
            bf(ny, rows, WIDE), bf(ny, rows, WIDE), bf(ny, rows, LANES),
            fl(BLOCK, HEADS_HERE * LANES), fl(HEADS_HERE, BLOCK), fl(BLOCK, BLOCK), fl(BLOCK, BLOCK),
            fl(BLOCK, BLOCK), bf(BLOCK, WIDE), bf(BLOCK, WIDE), fl(BLOCK, WIDE), fl(BLOCK, WIDE),
            pltpu.SemaphoreType.DMA((7, ny)), pltpu.SemaphoreType.DMA((7, ny)),
            pltpu.SemaphoreType.DMA((5, nz)), pltpu.SemaphoreType.DMA((5, nz)),
            pltpu.SemaphoreType.DMA((2, nx)), pltpu.SemaphoreType.DMA((2, nx)),
            pltpu.SemaphoreType.DMA((7,)), pltpu.SemaphoreType.REGULAR((4,)),
        ],
        compiler_params=pltpu.CompilerParams(collective_id=0, has_side_effects=True),
    )(inputs, step_sizes, decay_rates, state_write, state_read, doc_lengths, out_grad)
    return pl.pallas_call(
        functools.partial(last, ny),
        out_shape=(wide_shape, wide_shape, thin_shape, thin_shape),
        in_specs=[vmem, vmem, vmem],
        out_specs=(anywhere, anywhere, anywhere, anywhere),
        scratch_shapes=[bf(*state_write.shape), bf(*state_read.shape), pltpu.SemaphoreType.DMA((4,))],
    )(*[pltpu.with_memory_space_constraint(part, pltpu.VMEM) for part in outs])


def solution(mesh):
    nctx, ny = mesh.shape["ctx"], mesh.shape["head"]
    nz = 16 if nctx % 16 == 0 else nctx // 2
    nx = nctx // nz
    rows = P(("ctx", "head"), None)
    return jax.shard_map(
        functools.partial(on_device, nx, nz, ny),
        mesh=mesh,
        in_specs=(rows, rows, P("head"), rows, rows, P(), rows),
        out_specs=(rows, rows, rows, rows),
        check_vma=False,
    )
```

```python
import functools

import jax
import jax.numpy as jnp
from jax import lax
from jax.experimental import pallas as pl
from jax.experimental.pallas import tpu as pltpu
from jax.sharding import PartitionSpec as P

HEAD_DIM = 64
STATE = 64
BLOCK = 256
DOCS = 16
HEADS_HERE = 8
WIDE = HEADS_HERE * HEAD_DIM
PAIRS = HEADS_HERE // 2
LANES = 128
NEG = -1e30
F32 = jnp.float32
BF16 = jnp.bfloat16


def dot_nn(a, b):
    return lax.dot_general(a, b, (((1,), (0,)), ((), ())), preferred_element_type=F32)


def dot_nt(a, b):
    return lax.dot_general(a, b, (((1,), (1,)), ((), ())), preferred_element_type=F32)


def dot_tn(a, b):
    return lax.dot_general(a, b, (((0,), (0,)), ((), ())), preferred_element_type=F32)


def kernel(
    nx, nz, ny,
    x_ref, step_ref, rate_ref, w_ref, r_ref, doc_ref, g_ref,
    out_ref, dx_ref, gw_recv,
    x_in, g_in, step_in, w_in, r_in, rate_in, doc_in,
    sw_send, sw_buf, v_buf, g_buf,
    dec_send, dec_recv, f_send, f_recv, b_send, b_recv,
    xf_send, xf_recv, xb_send, xb_recv,
    rf_send, rf_recv, rb_send, rb_recv,
    out_send, dx_send, gw_send,
    run_col, run_row, bias_ref, score_ref, dscore_ref, ev_ref, cg_ref, loc_ref, dv_ref, fin_ref, fout_ref,
    y_ssem, y_rsem, z_ssem, z_rsem, x_ssem, x_rsem, own_sem, ready,
):
    rows = BLOCK // ny
    blocks_of = nz // PAIRS
    piece = STATE // blocks_of
    ctx = lax.axis_index("ctx")
    me = lax.axis_index("head")
    zme = lax.rem(ctx, nz)
    xme = lax.div(ctx, nz)
    base = xme * nz

    def y_peer(k):
        return lax.rem(me + k, ny)

    def z_peer(k):
        return lax.rem(zme + k, nz)

    def x_peer(k):
        return lax.rem(xme + k, nx)

    def y_copy(cat, k, src, dst):
        return pltpu.make_async_remote_copy(
            src_ref=src, dst_ref=dst, send_sem=y_ssem.at[cat], recv_sem=y_rsem.at[cat],
            device_id={"ctx": ctx, "head": y_peer(k)}, device_id_type=pl.DeviceIdType.MESH)

    def z_copy(cat, k, src, dst):
        return pltpu.make_async_remote_copy(
            src_ref=src, dst_ref=dst, send_sem=z_ssem.at[cat], recv_sem=z_rsem.at[cat],
            device_id={"ctx": base + z_peer(k), "head": me}, device_id_type=pl.DeviceIdType.MESH)

    def x_copy(cat, k, src, dst):
        return pltpu.make_async_remote_copy(
            src_ref=src, dst_ref=dst, send_sem=x_ssem.at[cat], recv_sem=x_rsem.at[cat],
            device_id={"ctx": x_peer(k) * nz + zme, "head": me}, device_id_type=pl.DeviceIdType.MESH)

    def signal_y(sem, k):
        pl.semaphore_signal(
            sem, inc=1, device_id={"ctx": ctx, "head": y_peer(k)}, device_id_type=pl.DeviceIdType.MESH)

    def signal_z(sem, k):
        pl.semaphore_signal(
            sem, inc=1, device_id={"ctx": base + z_peer(k), "head": me}, device_id_type=pl.DeviceIdType.MESH)

    def signal_x(sem, k):
        pl.semaphore_signal(
            sem, inc=1, device_id={"ctx": x_peer(k) * nz + zme, "head": me}, device_id_type=pl.DeviceIdType.MESH)

    def wide(at):
        return pl.ds(pl.multiple_of(at * WIDE, WIDE), WIDE)

    def far_first(n):
        return sorted(range(1, n), key=lambda k: (-min(k, n - k), k))

    def some(ref, n):
        return ref.at[pl.ds(0, n - 1)]

    def some_wide(ref):
        return ref.at[:, pl.ds(0, (ny - 1) * WIDE)]

    barrier = pltpu.get_barrier_semaphore()
    x_near = sorted({1, nx - 1})
    for k in far_first(ny):
        signal_y(barrier, k)
    for k in x_near:
        signal_x(barrier, k)
    for k in (1, nz - 1):
        signal_z(barrier, k)

    fetch = [
        pltpu.make_async_copy(src, dst, own_sem.at[i])
        for i, (src, dst) in enumerate((
            (step_ref, step_in), (w_ref, w_in), (r_ref, r_in), (x_ref, x_in), (g_ref, g_in),
            (doc_ref, doc_in), (rate_ref, rate_in)))
    ]
    for copy in fetch:
        copy.start()

    low = lax.broadcasted_iota(jnp.int32, (rows, LANES), 1) < 64
    for copy in fetch[0:3]:
        copy.wait()
    steps_here = step_in[...]
    if ny * HEADS_HERE < LANES:
        steps_here = jnp.concatenate([steps_here, jnp.zeros((rows, LANES - ny * HEADS_HERE), BF16)], axis=1)
    for pair in range(ny // 2):
        cols = slice(pair * LANES, (pair + 1) * LANES)
        w2 = w_in[:, cols].astype(F32)
        r2 = r_in[:, cols].astype(F32)
        sw_send[2 * pair, :, 0:LANES] = steps_here
        sw_send[2 * pair + 1, :, 0:LANES] = steps_here
        sw_send[2 * pair, :, LANES:2 * LANES] = jnp.where(low, w2, pltpu.roll(r2, 64, 1)).astype(BF16)
        sw_send[2 * pair + 1, :, LANES:2 * LANES] = jnp.where(low, pltpu.roll(w2, 64, 1), r2).astype(BF16)
    fetch[3].wait()
    pl.semaphore_wait(barrier, ny - 1 + len(x_near) + 2)

    steps_z = []
    radius = 1
    while radius < nz // 2:
        steps_z.append(radius)
        radius *= 2

    def reach_start(at):
        if at < len(steps_z):
            for k in (steps_z[at], nz - steps_z[at]):
                signal_z(ready.at[at], k)

    def reach_end(at):
        if at < len(steps_z):
            pl.semaphore_wait(ready.at[at], 2)

    reach_start(0)
    if nx > 2:
        signal_x(ready.at[3], 1)
        signal_x(ready.at[3], nx - 1)

    for k in far_first(ny):
        y_copy(0, k, sw_send.at[y_peer(k)], sw_buf.at[me]).start()
    for k in far_first(ny):
        y_copy(1, k, x_in.at[:, wide(y_peer(k))], v_buf.at[me]).start()
    reach_end(0)
    reach_start(1)
    fetch[4].wait()
    for k in far_first(ny):
        y_copy(2, k, g_in.at[:, wide(y_peer(k))], g_buf.at[me]).start()

    fetch[5].wait()
    fetch[6].wait()
    first = ctx * BLOCK
    starts, at = [], jnp.int32(0)
    for k in range(DOCS):
        starts.append(at)
        at = at + doc_in[k]

    def segment(pos):
        seg = jnp.where(starts[0] <= pos, 1, 0)
        for k in range(1, DOCS):
            seg = seg + jnp.where(starts[k] <= pos, 1, 0)
        return seg

    seg_before = segment(first - 1)
    seg_last = segment(first + BLOCK - 1)
    seg_col = segment(first + lax.broadcasted_iota(jnp.int32, (BLOCK, LANES), 0))
    seg_row = segment(first + lax.broadcasted_iota(jnp.int32, (8, BLOCK), 1))[0:1]
    if nx > 2:
        pl.semaphore_wait(ready.at[3], 2)
    reach_end(1)
    reach_start(2)
    v_buf[me] = x_in[:, wide(me)]
    g_buf[me] = g_in[:, wide(me)]
    sw_buf[me] = sw_send[me]
    row_i = lax.broadcasted_iota(jnp.int32, (BLOCK, BLOCK), 0)
    col_i = lax.broadcasted_iota(jnp.int32, (BLOCK, BLOCK), 1)
    causal = row_i >= col_i
    seg_wide = jnp.concatenate([seg_col, seg_col], axis=1)
    bias_ref[...] = jnp.where(causal & (seg_wide == seg_row), 0.0, NEG)
    dscore_ref[...] = jnp.zeros((BLOCK, BLOCK), F32)
    through = jnp.where(seg_last == seg_before, 1.0, 0.0)

    y_copy(0, 1, some(sw_send, ny), some(sw_buf, ny)).wait_recv()
    steps = sw_buf[:, :, 0:LANES].reshape(BLOCK, LANES)
    wr = sw_buf[:, :, LANES:2 * LANES].reshape(BLOCK, LANES)
    pick = (lax.broadcasted_iota(jnp.int32, (LANES, HEADS_HERE * LANES), 0) == me * HEADS_HERE
            + lax.broadcasted_iota(jnp.int32, (LANES, HEADS_HERE * LANES), 1) // LANES)
    spread_steps = dot_nn(steps, jnp.where(pick, 1.0, 0.0).astype(BF16)).astype(BF16)
    summed = dot_nn(jnp.where(causal, 1.0, 0.0).astype(BF16), spread_steps)
    pick_row = (lax.broadcasted_iota(jnp.int32, (16, LANES), 1) == me * HEADS_HERE
                + lax.broadcasted_iota(jnp.int32, (16, LANES), 0))
    steps_row = dot_nt(jnp.where(pick_row, 1.0, 0.0).astype(BF16), steps).astype(BF16)
    summed_row = dot_nn(steps_row, jnp.where(row_i <= col_i, 1.0, 0.0).astype(BF16))
    for h in range(HEADS_HERE):
        run_col[:, h * LANES:(h + 1) * LANES] = summed[:, h * LANES:(h + 1) * LANES] * (-rate_in[h])
        run_row[h:h + 1, :] = summed_row[h:h + 1, :] * (-rate_in[h])
    low = lax.broadcasted_iota(jnp.int32, (BLOCK, LANES), 1) < 64
    low_row = low[0:1]

    def pair_run(t):
        return jnp.where(low, run_col[:, 2 * t * LANES:(2 * t + 1) * LANES],
                         run_col[:, (2 * t + 1) * LANES:(2 * t + 2) * LANES])

    def pair_last(t):
        return jnp.where(low_row, run_col[BLOCK - 1:BLOCK, 2 * t * LANES:(2 * t + 1) * LANES],
                         run_col[BLOCK - 1:BLOCK, (2 * t + 1) * LANES:(2 * t + 2) * LANES])

    def factor_in(t):
        return jnp.where(seg_col == seg_before, jnp.exp(pair_run(t)), 0.0)

    def factor_out(t):
        return jnp.where(seg_col == seg_last, jnp.exp(pair_last(t) - pair_run(t)), 0.0)

    for t in range(PAIRS):
        dec_send[t] = jnp.exp(pair_last(t)) * through
    dec_recv[zme] = dec_send[zme // blocks_of]
    reach_end(2)
    for k in far_first(nz):
        z_copy(0, k, dec_send.at[lax.div(z_peer(k), blocks_of)], dec_recv.at[zme]).start()

    for t in range(PAIRS):
        cols = slice(t * LANES, (t + 1) * LANES)
        fout_ref[:, cols] = factor_out(t)
        fin_ref[:, cols] = factor_in(t)
    rw = pltpu.roll(wr.astype(F32), 64, 1)
    writers = wr[:, 0:64]
    readers = rw[:, 0:64].astype(BF16)
    read_low = jnp.where(low, rw, 0.0).astype(BF16)
    write_high = jnp.where(low, 0.0, rw).astype(BF16)
    score_ref[...] = dot_nt(readers, writers)
    turned = jnp.transpose(wr.astype(F32)).astype(BF16)

    y_copy(1, 1, some_wide(x_in), some(v_buf, ny)).wait_recv()
    for t in range(PAIRS):
        cols = slice(t * LANES, (t + 1) * LANES)
        values = v_buf[:, :, cols].reshape(BLOCK, LANES)
        ev = (values.astype(F32) * fout_ref[:, cols]).astype(BF16)
        ev_ref[:, cols] = ev
        added = dot_nn(turned[0:STATE], ev).astype(BF16)
        f_send[t * blocks_of:(t + 1) * blocks_of] = added.reshape(blocks_of, piece, LANES)
    for k in far_first(nz):
        z_copy(1, k, f_send.at[z_peer(k)], f_recv.at[zme]).start()
    f_recv[zme] = f_send[zme]

    y_copy(2, 1, some_wide(g_in), some(g_buf, ny)).wait_recv()
    for t in range(PAIRS):
        cols = slice(t * LANES, (t + 1) * LANES)
        grads = g_buf[:, :, cols].reshape(BLOCK, LANES)
        cg = (grads.astype(F32) * fin_ref[:, cols]).astype(BF16)
        cg_ref[:, cols] = cg
        added = dot_nn(turned[STATE:2 * STATE], cg).astype(BF16)
        b_send[t * blocks_of:(t + 1) * blocks_of] = added.reshape(blocks_of, piece, LANES)
    for k in far_first(nz):
        z_copy(2, k, b_send.at[z_peer(k)], b_recv.at[zme]).start()
    b_recv[zme] = b_send[zme]

    low_one = jnp.where(low_row, 1.0, 0.0).astype(BF16)
    high_one = jnp.where(low_row, 0.0, 1.0).astype(BF16)

    def inside(t, carry):
        cols = pl.ds(pl.multiple_of(t * LANES, LANES), LANES)
        values = v_buf[:, :, cols].reshape(BLOCK, LANES)
        grads = g_buf[:, :, cols].reshape(BLOCK, LANES)
        local = jnp.zeros((BLOCK, LANES), F32)
        dvalue = jnp.zeros((BLOCK, LANES), F32)
        for half, ones in ((0, low_one), (1, high_one)):
            h = 2 * t + half
            column = run_col[:, pl.ds(pl.multiple_of(h * LANES, LANES), LANES)]
            row = run_row[pl.ds(h, 1), :]
            factor = jnp.exp(jnp.concatenate([column, column], axis=1) - row + bias_ref[...])
            weights = (score_ref[...] * factor).astype(BF16)
            half_grads = grads * ones
            local = local + dot_nn(weights, values * ones)
            dscore_ref[...] += dot_nt(half_grads, values) * factor
            dvalue = dvalue + dot_tn(weights, half_grads)
        loc_ref[:, cols] = local
        dv_ref[:, cols] = dvalue
        return carry

    lax.fori_loop(0, 2, inside, 0)

    z_copy(0, 1, some(dec_recv, nz), some(dec_recv, nz)).wait_recv()
    z_copy(1, 1, some(f_send, nz), some(f_recv, nz)).wait_recv()
    total = jnp.zeros((piece, LANES), F32)
    product = jnp.ones((1, LANES), F32)
    for z in range(nz):
        total = dec_recv[z] * total + f_recv[z].astype(F32)
        product = dec_recv[z] * product
    xf_send[0:piece] = total
    xf_send[piece:piece + 8] = jnp.broadcast_to(product, (8, LANES))
    for k in far_first(nx):
        x_copy(0, k, xf_send, xf_recv.at[xme]).start()
    xf_recv[xme] = xf_send[...]
    z_copy(2, 1, some(b_send, nz), some(b_recv, nz)).wait_recv()
    total = jnp.zeros((piece, LANES), F32)
    for z in reversed(range(nz)):
        total = dec_recv[z] * total + b_recv[z].astype(F32)
    xb_send[...] = total
    for k in far_first(nx):
        x_copy(1, k, xb_send, xb_recv.at[xme]).start()
    xb_recv[xme] = xb_send[...]

    lax.fori_loop(2, 3, inside, 0)

    x_copy(0, 1, some(xf_recv, nx), some(xf_recv, nx)).wait_recv()
    state = jnp.zeros((piece, LANES), F32)
    for x in range(nx):
        longer = xf_recv[x, piece:piece + 1] * state + xf_recv[x, 0:piece]
        state = jnp.where(x < xme, longer, state)
    for z in range(nz):
        rf_send[z] = state.astype(BF16)
        state = dec_recv[z] * state + f_recv[z].astype(F32)
    for k in far_first(nz):
        z_copy(3, k, rf_send.at[z_peer(k)], rf_recv.at[zme]).start()
    rf_recv[zme] = rf_send[zme]

    x_copy(1, 1, some(xb_recv, nx), some(xb_recv, nx)).wait_recv()
    state = jnp.zeros((piece, LANES), F32)
    for x in reversed(range(nx)):
        longer = xf_recv[x, piece:piece + 1] * state + xb_recv[x]
        state = jnp.where(x > xme, longer, state)
    for z in reversed(range(nz)):
        rb_send[z] = state.astype(BF16)
        state = dec_recv[z] * state + b_recv[z].astype(F32)
    for k in far_first(nz):
        z_copy(4, k, rb_send.at[z_peer(k)], rb_recv.at[zme]).start()
    rb_recv[zme] = rb_send[zme]

    lax.fori_loop(3, 4, inside, 0)
    dscore = dscore_ref[...].astype(BF16)
    gw = dot_nn(dscore, write_high) + dot_tn(dscore, read_low)
    nothing = jnp.zeros((STATE, LANES), BF16)

    z_copy(3, 1, some(rf_send, nz), some(rf_recv, nz)).wait_recv()
    for t in range(PAIRS):
        cols = slice(t * LANES, (t + 1) * LANES)
        entering = rf_recv[t * blocks_of:(t + 1) * blocks_of].reshape(STATE, LANES)
        result = loc_ref[:, cols] + fin_ref[:, cols] * dot_nn(readers, entering)
        out_send[:, :, cols] = result.astype(BF16).reshape(ny, rows, LANES)
    for k in far_first(ny):
        y_copy(3, k, out_send.at[y_peer(k)], out_ref.at[:, wide(me)]).start()
    out_ref[:, wide(me)] = out_send[me]
    for t in range(PAIRS):
        cols = slice(t * LANES, (t + 1) * LANES)
        entering = rf_recv[t * blocks_of:(t + 1) * blocks_of].reshape(STATE, LANES)
        gw = gw + dot_nt(cg_ref[:, cols], jnp.concatenate([nothing, entering], axis=0))

    z_copy(4, 1, some(rb_send, nz), some(rb_recv, nz)).wait_recv()
    for t in range(PAIRS):
        cols = slice(t * LANES, (t + 1) * LANES)
        leaving = rb_recv[t * blocks_of:(t + 1) * blocks_of].reshape(STATE, LANES)
        result = dv_ref[:, cols] + fout_ref[:, cols] * dot_nn(writers, leaving)
        dx_send[:, :, cols] = result.astype(BF16).reshape(ny, rows, LANES)
    for k in far_first(ny):
        y_copy(4, k, dx_send.at[y_peer(k)], dx_ref.at[:, wide(me)]).start()
    dx_ref[:, wide(me)] = dx_send[me]
    for t in range(PAIRS):
        cols = slice(t * LANES, (t + 1) * LANES)
        leaving = rb_recv[t * blocks_of:(t + 1) * blocks_of].reshape(STATE, LANES)
        gw = gw + dot_nt(ev_ref[:, cols], jnp.concatenate([leaving, nothing], axis=0))
    gw_send[...] = gw.astype(BF16).reshape(ny, rows, LANES)
    for k in far_first(ny):
        y_copy(5, k, gw_send.at[y_peer(k)], gw_recv.at[me]).start()
    gw_recv[me] = gw_send[me]

    y_copy(0, 1, some(sw_send, ny), some(sw_buf, ny)).wait_send()
    y_copy(1, 1, some_wide(x_in), some(v_buf, ny)).wait_send()
    y_copy(2, 1, some_wide(g_in), some(g_buf, ny)).wait_send()
    z_copy(0, 1, some(dec_recv, nz), some(dec_recv, nz)).wait_send()
    z_copy(1, 1, some(f_send, nz), some(f_recv, nz)).wait_send()
    z_copy(2, 1, some(b_send, nz), some(b_recv, nz)).wait_send()
    z_copy(3, 1, some(rf_send, nz), some(rf_recv, nz)).wait_send()
    z_copy(4, 1, some(rb_send, nz), some(rb_recv, nz)).wait_send()
    x_copy(0, 1, some(xf_recv, nx), some(xf_recv, nx)).wait_send()
    x_copy(1, 1, some(xb_recv, nx), some(xb_recv, nx)).wait_send()
    y_copy(3, 1, some(out_send, ny), some_wide(out_ref)).wait()
    y_copy(4, 1, some(dx_send, ny), some_wide(dx_ref)).wait()
    y_copy(5, 1, some(gw_send, ny), some(gw_recv, ny)).wait()


def last(ny, out_in, dx_in, gw_in, out_ref, dx_ref, dw_ref, dr_ref, dw_out, dr_out, sem):
    rows = BLOCK // ny
    out_copy = pltpu.make_async_copy(out_in, out_ref, sem.at[0])
    dx_copy = pltpu.make_async_copy(dx_in, dx_ref, sem.at[1])
    dw_copy = pltpu.make_async_copy(dw_out, dw_ref, sem.at[2])
    dr_copy = pltpu.make_async_copy(dr_out, dr_ref, sem.at[3])
    out_copy.start()
    dx_copy.start()
    low = lax.broadcasted_iota(jnp.int32, (rows, LANES), 1) < 64
    for pair in range(ny // 2):
        cols = slice(pair * LANES, (pair + 1) * LANES)
        even = gw_in[2 * pair].astype(F32)
        odd = gw_in[2 * pair + 1].astype(F32)
        dw_out[:, cols] = jnp.where(low, even, pltpu.roll(odd, 64, 1)).astype(BF16)
        dr_out[:, cols] = jnp.where(low, pltpu.roll(even, 64, 1), odd).astype(BF16)
    dw_copy.start()
    dr_copy.start()
    out_copy.wait()
    dx_copy.wait()
    dw_copy.wait()
    dr_copy.wait()


def on_device(nx, nz, ny, inputs, step_sizes, decay_rates, state_write, state_read, doc_lengths, out_grad):
    rows = BLOCK // ny
    piece = STATE // (nz // PAIRS)
    vmem = pl.BlockSpec(memory_space=pltpu.VMEM)
    anywhere = pl.BlockSpec(memory_space=pl.ANY)
    wide_shape = jax.ShapeDtypeStruct(inputs.shape, BF16)
    thin_shape = jax.ShapeDtypeStruct(state_write.shape, BF16)
    bf = lambda *shape: pltpu.VMEM(shape, BF16)
    fl = lambda *shape: pltpu.VMEM(shape, F32)
    outs = pl.pallas_call(
        functools.partial(kernel, nx, nz, ny),
        out_shape=(bf(*inputs.shape), bf(*inputs.shape), bf(ny, rows, LANES)),
        in_specs=[anywhere] * 7,
        out_specs=(vmem, vmem, vmem),
        scratch_shapes=[
            bf(rows, ny * WIDE), bf(rows, ny * WIDE), bf(*step_sizes.shape), bf(*state_write.shape),
            bf(*state_read.shape), pltpu.SMEM(decay_rates.shape, F32), pltpu.SMEM((DOCS,), jnp.int32),
            bf(ny, rows, 2 * LANES), bf(ny, rows, 2 * LANES),
            bf(ny, rows, WIDE), bf(ny, rows, WIDE),
            fl(PAIRS, 1, LANES), fl(nz, 1, LANES),
            bf(nz, piece, LANES), bf(nz, piece, LANES), bf(nz, piece, LANES), bf(nz, piece, LANES),
            fl(piece + 8, LANES), fl(nx, piece + 8, LANES), fl(piece, LANES), fl(nx, piece, LANES),
            bf(nz, piece, LANES), bf(nz, piece, LANES), bf(nz, piece, LANES), bf(nz, piece, LANES),
            bf(ny, rows, WIDE), bf(ny, rows, WIDE), bf(ny, rows, LANES),
            fl(BLOCK, HEADS_HERE * LANES), fl(HEADS_HERE, BLOCK), fl(BLOCK, BLOCK), fl(BLOCK, BLOCK),
            fl(BLOCK, BLOCK), bf(BLOCK, WIDE), bf(BLOCK, WIDE), fl(BLOCK, WIDE), fl(BLOCK, WIDE),
            fl(BLOCK, WIDE), fl(BLOCK, WIDE),
            pltpu.SemaphoreType.DMA((6,)), pltpu.SemaphoreType.DMA((6,)),
            pltpu.SemaphoreType.DMA((5,)), pltpu.SemaphoreType.DMA((5,)),
            pltpu.SemaphoreType.DMA((2,)), pltpu.SemaphoreType.DMA((2,)),
            pltpu.SemaphoreType.DMA((7,)), pltpu.SemaphoreType.REGULAR((4,)),
        ],
        compiler_params=pltpu.CompilerParams(collective_id=0, has_side_effects=True),
    )(inputs, step_sizes, decay_rates, state_write, state_read, doc_lengths, out_grad)
    return pl.pallas_call(
        functools.partial(last, ny),
        out_shape=(wide_shape, wide_shape, thin_shape, thin_shape),
        in_specs=[vmem, vmem, vmem],
        out_specs=(anywhere, anywhere, anywhere, anywhere),
        scratch_shapes=[bf(*state_write.shape), bf(*state_read.shape), pltpu.SemaphoreType.DMA((4,))],
    )(*[pltpu.with_memory_space_constraint(part, pltpu.VMEM) for part in outs])


def solution(mesh):
    nctx, ny = mesh.shape["ctx"], mesh.shape["head"]
    nz = 16 if nctx % 16 == 0 else nctx // 2
    nx = nctx // nz
    rows = P(("ctx", "head"), None)
    return jax.shard_map(
        functools.partial(on_device, nx, nz, ny),
        mesh=mesh,
        in_specs=(rows, rows, P("head"), rows, rows, P(), rows),
        out_specs=(rows, rows, rows, rows),
        check_vma=False,
    )
```

```python
import functools

import jax
import jax.numpy as jnp
from jax import lax
from jax.experimental import pallas as pl
from jax.experimental.pallas import tpu as pltpu
from jax.sharding import PartitionSpec as P

HEAD_DIM = 64
STATE = 64
BLOCK = 256
DOCS = 16
HEADS_HERE = 8
WIDE = HEADS_HERE * HEAD_DIM
PAIRS = HEADS_HERE // 2
LANES = 128
NEG = -1e30
F32 = jnp.float32
BF16 = jnp.bfloat16


def dot_nn(a, b):
    return lax.dot_general(a, b, (((1,), (0,)), ((), ())), preferred_element_type=F32)


def dot_nt(a, b):
    return lax.dot_general(a, b, (((1,), (1,)), ((), ())), preferred_element_type=F32)


def dot_tn(a, b):
    return lax.dot_general(a, b, (((0,), (0,)), ((), ())), preferred_element_type=F32)


def kernel(
    nx, nz, ny,
    x_ref, step_ref, rate_ref, w_ref, r_ref, doc_ref, g_ref,
    out_ref, dx_ref, gw_recv,
    step_in, w_in, r_in, rate_in, doc_in,
    sw_send, sw_buf, v_buf, g_buf,
    dec_send, dec_recv, f_send, f_recv, b_send, b_recv,
    xf_send, xf_recv, xb_send, xb_recv,
    rf_send, rf_recv, rb_send, rb_recv,
    out_send, dx_send, gw_send,
    run_col, run_row, bias_ref, score_ref, dscore_ref, ev_ref, cg_ref, loc_ref, dv_ref, fin_ref, fout_ref,
    y_ssem, y_rsem, z_ssem, z_rsem, x_ssem, x_rsem, own_sem, ready,
):
    rows = BLOCK // ny
    blocks_of = nz // PAIRS
    piece = STATE // blocks_of
    ctx = lax.axis_index("ctx")
    me = lax.axis_index("head")
    zme = lax.rem(ctx, nz)
    xme = lax.div(ctx, nz)
    base = xme * nz

    def y_peer(k):
        return lax.rem(me + k, ny)

    def z_peer(k):
        return lax.rem(zme + k, nz)

    def x_peer(k):
        return lax.rem(xme + k, nx)

    def y_copy(cat, k, src, dst):
        return pltpu.make_async_remote_copy(
            src_ref=src, dst_ref=dst, send_sem=y_ssem.at[cat], recv_sem=y_rsem.at[cat],
            device_id={"ctx": ctx, "head": y_peer(k)}, device_id_type=pl.DeviceIdType.MESH)

    def z_copy(cat, k, src, dst):
        return pltpu.make_async_remote_copy(
            src_ref=src, dst_ref=dst, send_sem=z_ssem.at[cat], recv_sem=z_rsem.at[cat],
            device_id={"ctx": base + z_peer(k), "head": me}, device_id_type=pl.DeviceIdType.MESH)

    def x_copy(cat, k, src, dst):
        return pltpu.make_async_remote_copy(
            src_ref=src, dst_ref=dst, send_sem=x_ssem.at[cat], recv_sem=x_rsem.at[cat],
            device_id={"ctx": x_peer(k) * nz + zme, "head": me}, device_id_type=pl.DeviceIdType.MESH)

    def signal_y(sem, k):
        pl.semaphore_signal(
            sem, inc=1, device_id={"ctx": ctx, "head": y_peer(k)}, device_id_type=pl.DeviceIdType.MESH)

    def signal_z(sem, k):
        pl.semaphore_signal(
            sem, inc=1, device_id={"ctx": base + z_peer(k), "head": me}, device_id_type=pl.DeviceIdType.MESH)

    def signal_x(sem, k):
        pl.semaphore_signal(
            sem, inc=1, device_id={"ctx": x_peer(k) * nz + zme, "head": me}, device_id_type=pl.DeviceIdType.MESH)

    def wide(at):
        return pl.ds(pl.multiple_of(at * WIDE, WIDE), WIDE)

    def far_first(n):
        return sorted(range(1, n), key=lambda k: (-min(k, n - k), k))

    def near_first(n):
        return far_first(n)[::-1]

    def some(ref, n):
        return ref.at[pl.ds(0, n - 1)]

    def some_wide(ref):
        return ref.at[:, pl.ds(0, (ny - 1) * WIDE)]

    barrier = pltpu.get_barrier_semaphore()
    x_near = sorted({1, nx - 1})
    for k in far_first(ny):
        signal_y(barrier, k)
    for k in x_near:
        signal_x(barrier, k)
    for k in (1, nz - 1):
        signal_z(barrier, k)

    fetch = [
        pltpu.make_async_copy(src, dst, own_sem.at[i])
        for i, (src, dst) in enumerate((
            (step_ref, step_in), (w_ref, w_in), (r_ref, r_in), (x_ref.at[:, wide(me)], v_buf.at[me]),
            (g_ref.at[:, wide(me)], g_buf.at[me]),
            (doc_ref, doc_in), (rate_ref, rate_in)))
    ]
    for copy in fetch:
        copy.start()

    low = lax.broadcasted_iota(jnp.int32, (rows, LANES), 1) < 64
    for copy in fetch[0:3]:
        copy.wait()
    steps_here = step_in[...]
    if ny * HEADS_HERE < LANES:
        steps_here = jnp.concatenate([steps_here, jnp.zeros((rows, LANES - ny * HEADS_HERE), BF16)], axis=1)
    for pair in range(ny // 2):
        cols = slice(pair * LANES, (pair + 1) * LANES)
        w2 = w_in[:, cols].astype(F32)
        r2 = r_in[:, cols].astype(F32)
        sw_send[2 * pair, :, 0:LANES] = steps_here
        sw_send[2 * pair + 1, :, 0:LANES] = steps_here
        sw_send[2 * pair, :, LANES:2 * LANES] = jnp.where(low, w2, pltpu.roll(r2, 64, 1)).astype(BF16)
        sw_send[2 * pair + 1, :, LANES:2 * LANES] = jnp.where(low, pltpu.roll(w2, 64, 1), r2).astype(BF16)
    pl.semaphore_wait(barrier, ny - 1 + len(x_near) + 2)

    steps_z = []
    radius = 1
    while radius < nz // 2:
        steps_z.append(radius)
        radius *= 2

    def reach_start(at):
        if at < len(steps_z):
            for k in (steps_z[at], nz - steps_z[at]):
                signal_z(ready.at[at], k)

    def reach_end(at):
        if at < len(steps_z):
            pl.semaphore_wait(ready.at[at], 2)

    reach_start(0)
    if nx > 2:
        signal_x(ready.at[3], 1)
        signal_x(ready.at[3], nx - 1)

    for k in near_first(ny):
        y_copy(0, k, sw_send.at[y_peer(k)], sw_buf.at[me]).start()
    for k in near_first(ny):
        y_copy(1, k, x_ref.at[:, wide(y_peer(k))], v_buf.at[me]).start()
    reach_end(0)
    reach_start(1)
    for k in near_first(ny):
        y_copy(2, k, g_ref.at[:, wide(y_peer(k))], g_buf.at[me]).start()

    fetch[5].wait()
    fetch[6].wait()
    first = ctx * BLOCK
    starts, at = [], jnp.int32(0)
    for k in range(DOCS):
        starts.append(at)
        at = at + doc_in[k]

    def segment(pos):
        seg = jnp.where(starts[0] <= pos, 1, 0)
        for k in range(1, DOCS):
            seg = seg + jnp.where(starts[k] <= pos, 1, 0)
        return seg

    seg_before = segment(first - 1)
    seg_last = segment(first + BLOCK - 1)
    seg_col = segment(first + lax.broadcasted_iota(jnp.int32, (BLOCK, LANES), 0))
    seg_row = segment(first + lax.broadcasted_iota(jnp.int32, (8, BLOCK), 1))[0:1]
    if nx > 2:
        pl.semaphore_wait(ready.at[3], 2)
    reach_end(1)
    reach_start(2)
    fetch[3].wait()
    fetch[4].wait()
    sw_buf[me] = sw_send[me]
    row_i = lax.broadcasted_iota(jnp.int32, (BLOCK, BLOCK), 0)
    col_i = lax.broadcasted_iota(jnp.int32, (BLOCK, BLOCK), 1)
    causal = row_i >= col_i
    seg_wide = jnp.concatenate([seg_col, seg_col], axis=1)
    bias_ref[...] = jnp.where(causal & (seg_wide == seg_row), 0.0, NEG)
    dscore_ref[...] = jnp.zeros((BLOCK, BLOCK), F32)
    through = jnp.where(seg_last == seg_before, 1.0, 0.0)

    y_copy(0, 1, some(sw_send, ny), some(sw_buf, ny)).wait_recv()
    steps = sw_buf[:, :, 0:LANES].reshape(BLOCK, LANES)
    wr = sw_buf[:, :, LANES:2 * LANES].reshape(BLOCK, LANES)
    pick = (lax.broadcasted_iota(jnp.int32, (LANES, HEADS_HERE * LANES), 0) == me * HEADS_HERE
            + lax.broadcasted_iota(jnp.int32, (LANES, HEADS_HERE * LANES), 1) // LANES)
    spread_steps = dot_nn(steps, jnp.where(pick, 1.0, 0.0).astype(BF16)).astype(BF16)
    summed = dot_nn(jnp.where(causal, 1.0, 0.0).astype(BF16), spread_steps)
    pick_row = (lax.broadcasted_iota(jnp.int32, (16, LANES), 1) == me * HEADS_HERE
                + lax.broadcasted_iota(jnp.int32, (16, LANES), 0))
    steps_row = dot_nt(jnp.where(pick_row, 1.0, 0.0).astype(BF16), steps).astype(BF16)
    summed_row = dot_nn(steps_row, jnp.where(row_i <= col_i, 1.0, 0.0).astype(BF16))
    for h in range(HEADS_HERE):
        run_col[:, h * LANES:(h + 1) * LANES] = summed[:, h * LANES:(h + 1) * LANES] * (-rate_in[h])
        run_row[h:h + 1, :] = summed_row[h:h + 1, :] * (-rate_in[h])
    low = lax.broadcasted_iota(jnp.int32, (BLOCK, LANES), 1) < 64
    low_row = low[0:1]

    def pair_run(t):
        return jnp.where(low, run_col[:, 2 * t * LANES:(2 * t + 1) * LANES],
                         run_col[:, (2 * t + 1) * LANES:(2 * t + 2) * LANES])

    def pair_last(t):
        return jnp.where(low_row, run_col[BLOCK - 1:BLOCK, 2 * t * LANES:(2 * t + 1) * LANES],
                         run_col[BLOCK - 1:BLOCK, (2 * t + 1) * LANES:(2 * t + 2) * LANES])

    def factor_in(t):
        return jnp.where(seg_col == seg_before, jnp.exp(pair_run(t)), 0.0)

    def factor_out(t):
        return jnp.where(seg_col == seg_last, jnp.exp(pair_last(t) - pair_run(t)), 0.0)

    for t in range(PAIRS):
        dec_send[t] = jnp.exp(pair_last(t)) * through
    dec_recv[zme] = dec_send[zme // blocks_of]
    reach_end(2)
    for k in far_first(nz):
        z_copy(0, k, dec_send.at[lax.div(z_peer(k), blocks_of)], dec_recv.at[zme]).start()

    for t in range(PAIRS):
        cols = slice(t * LANES, (t + 1) * LANES)
        fout_ref[:, cols] = factor_out(t)
        fin_ref[:, cols] = factor_in(t)
    rw = pltpu.roll(wr.astype(F32), 64, 1)
    writers = wr[:, 0:64]
    readers = rw[:, 0:64].astype(BF16)
    read_low = jnp.where(low, rw, 0.0).astype(BF16)
    write_high = jnp.where(low, 0.0, rw).astype(BF16)
    score_ref[...] = dot_nt(readers, writers)
    turned = jnp.transpose(wr.astype(F32)).astype(BF16)

    y_copy(1, 1, some_wide(x_ref), some(v_buf, ny)).wait_recv()
    for t in range(PAIRS):
        cols = slice(t * LANES, (t + 1) * LANES)
        values = v_buf[:, :, cols].reshape(BLOCK, LANES)
        ev = (values.astype(F32) * fout_ref[:, cols]).astype(BF16)
        ev_ref[:, cols] = ev
        added = dot_nn(turned[0:STATE], ev).astype(BF16)
        f_send[t * blocks_of:(t + 1) * blocks_of] = added.reshape(blocks_of, piece, LANES)
    for k in far_first(nz):
        z_copy(1, k, f_send.at[z_peer(k)], f_recv.at[zme]).start()
    f_recv[zme] = f_send[zme]

    y_copy(2, 1, some_wide(g_ref), some(g_buf, ny)).wait_recv()
    for t in range(PAIRS):
        cols = slice(t * LANES, (t + 1) * LANES)
        grads = g_buf[:, :, cols].reshape(BLOCK, LANES)
        cg = (grads.astype(F32) * fin_ref[:, cols]).astype(BF16)
        cg_ref[:, cols] = cg
        added = dot_nn(turned[STATE:2 * STATE], cg).astype(BF16)
        b_send[t * blocks_of:(t + 1) * blocks_of] = added.reshape(blocks_of, piece, LANES)
    for k in far_first(nz):
        z_copy(2, k, b_send.at[z_peer(k)], b_recv.at[zme]).start()
    b_recv[zme] = b_send[zme]

    low_one = jnp.where(low_row, 1.0, 0.0).astype(BF16)
    high_one = jnp.where(low_row, 0.0, 1.0).astype(BF16)

    def inside(t, carry):
        cols = pl.ds(pl.multiple_of(t * LANES, LANES), LANES)
        values = v_buf[:, :, cols].reshape(BLOCK, LANES)
        grads = g_buf[:, :, cols].reshape(BLOCK, LANES)
        local = jnp.zeros((BLOCK, LANES), F32)
        dvalue = jnp.zeros((BLOCK, LANES), F32)
        for half, ones in ((0, low_one), (1, high_one)):
            h = 2 * t + half
            column = run_col[:, pl.ds(pl.multiple_of(h * LANES, LANES), LANES)]
            row = run_row[pl.ds(h, 1), :]
            factor = jnp.exp(jnp.concatenate([column, column], axis=1) - row + bias_ref[...])
            weights = (score_ref[...] * factor).astype(BF16)
            half_grads = grads * ones
            local = local + dot_nn(weights, values * ones)
            dscore_ref[...] += dot_nt(half_grads, values) * factor
            dvalue = dvalue + dot_tn(weights, half_grads)
        loc_ref[:, cols] = local
        dv_ref[:, cols] = dvalue
        return carry

    lax.fori_loop(0, 4, inside, 0)

    z_copy(0, 1, some(dec_recv, nz), some(dec_recv, nz)).wait_recv()
    z_copy(1, 1, some(f_send, nz), some(f_recv, nz)).wait_recv()
    total = jnp.zeros((piece, LANES), F32)
    product = jnp.ones((1, LANES), F32)
    for z in range(nz):
        total = dec_recv[z] * total + f_recv[z].astype(F32)
        product = dec_recv[z] * product
    xf_send[0:piece] = total
    xf_send[piece:piece + 8] = jnp.broadcast_to(product, (8, LANES))
    for k in far_first(nx):
        x_copy(0, k, xf_send, xf_recv.at[xme]).start()
    xf_recv[xme] = xf_send[...]
    z_copy(2, 1, some(b_send, nz), some(b_recv, nz)).wait_recv()
    total = jnp.zeros((piece, LANES), F32)
    for z in reversed(range(nz)):
        total = dec_recv[z] * total + b_recv[z].astype(F32)
    xb_send[...] = total
    for k in far_first(nx):
        x_copy(1, k, xb_send, xb_recv.at[xme]).start()
    xb_recv[xme] = xb_send[...]


    x_copy(0, 1, some(xf_recv, nx), some(xf_recv, nx)).wait_recv()
    state = jnp.zeros((piece, LANES), F32)
    for x in range(nx):
        longer = xf_recv[x, piece:piece + 1] * state + xf_recv[x, 0:piece]
        state = jnp.where(x < xme, longer, state)
    for z in range(nz):
        rf_send[z] = state.astype(BF16)
        state = dec_recv[z] * state + f_recv[z].astype(F32)
    for k in far_first(nz):
        z_copy(3, k, rf_send.at[z_peer(k)], rf_recv.at[zme]).start()
    rf_recv[zme] = rf_send[zme]

    x_copy(1, 1, some(xb_recv, nx), some(xb_recv, nx)).wait_recv()
    state = jnp.zeros((piece, LANES), F32)
    for x in reversed(range(nx)):
        longer = xf_recv[x, piece:piece + 1] * state + xb_recv[x]
        state = jnp.where(x > xme, longer, state)
    for z in reversed(range(nz)):
        rb_send[z] = state.astype(BF16)
        state = dec_recv[z] * state + b_recv[z].astype(F32)
    for k in far_first(nz):
        z_copy(4, k, rb_send.at[z_peer(k)], rb_recv.at[zme]).start()
    rb_recv[zme] = rb_send[zme]

    dscore = dscore_ref[...].astype(BF16)
    gw = dot_nn(dscore, write_high) + dot_tn(dscore, read_low)
    nothing = jnp.zeros((STATE, LANES), BF16)

    z_copy(3, 1, some(rf_send, nz), some(rf_recv, nz)).wait_recv()
    for t in range(PAIRS):
        cols = slice(t * LANES, (t + 1) * LANES)
        entering = rf_recv[t * blocks_of:(t + 1) * blocks_of].reshape(STATE, LANES)
        result = loc_ref[:, cols] + fin_ref[:, cols] * dot_nn(readers, entering)
        out_send[:, :, cols] = result.astype(BF16).reshape(ny, rows, LANES)
    for k in far_first(ny):
        y_copy(3, k, out_send.at[y_peer(k)], out_ref.at[:, wide(me)]).start()
    out_ref[:, wide(me)] = out_send[me]
    for t in range(PAIRS):
        cols = slice(t * LANES, (t + 1) * LANES)
        entering = rf_recv[t * blocks_of:(t + 1) * blocks_of].reshape(STATE, LANES)
        gw = gw + dot_nt(cg_ref[:, cols], jnp.concatenate([nothing, entering], axis=0))

    z_copy(4, 1, some(rb_send, nz), some(rb_recv, nz)).wait_recv()
    for t in range(PAIRS):
        cols = slice(t * LANES, (t + 1) * LANES)
        leaving = rb_recv[t * blocks_of:(t + 1) * blocks_of].reshape(STATE, LANES)
        result = dv_ref[:, cols] + fout_ref[:, cols] * dot_nn(writers, leaving)
        dx_send[:, :, cols] = result.astype(BF16).reshape(ny, rows, LANES)
    for k in far_first(ny):
        y_copy(4, k, dx_send.at[y_peer(k)], dx_ref.at[:, wide(me)]).start()
    dx_ref[:, wide(me)] = dx_send[me]
    for t in range(PAIRS):
        cols = slice(t * LANES, (t + 1) * LANES)
        leaving = rb_recv[t * blocks_of:(t + 1) * blocks_of].reshape(STATE, LANES)
        gw = gw + dot_nt(ev_ref[:, cols], jnp.concatenate([leaving, nothing], axis=0))
    gw_send[...] = gw.astype(BF16).reshape(ny, rows, LANES)
    for k in far_first(ny):
        y_copy(5, k, gw_send.at[y_peer(k)], gw_recv.at[me]).start()
    gw_recv[me] = gw_send[me]

    y_copy(0, 1, some(sw_send, ny), some(sw_buf, ny)).wait_send()
    y_copy(1, 1, some_wide(x_ref), some(v_buf, ny)).wait_send()
    y_copy(2, 1, some_wide(g_ref), some(g_buf, ny)).wait_send()
    z_copy(0, 1, some(dec_recv, nz), some(dec_recv, nz)).wait_send()
    z_copy(1, 1, some(f_send, nz), some(f_recv, nz)).wait_send()
    z_copy(2, 1, some(b_send, nz), some(b_recv, nz)).wait_send()
    z_copy(3, 1, some(rf_send, nz), some(rf_recv, nz)).wait_send()
    z_copy(4, 1, some(rb_send, nz), some(rb_recv, nz)).wait_send()
    x_copy(0, 1, some(xf_recv, nx), some(xf_recv, nx)).wait_send()
    x_copy(1, 1, some(xb_recv, nx), some(xb_recv, nx)).wait_send()
    y_copy(3, 1, some(out_send, ny), some_wide(out_ref)).wait()
    y_copy(4, 1, some(dx_send, ny), some_wide(dx_ref)).wait()
    y_copy(5, 1, some(gw_send, ny), some(gw_recv, ny)).wait()


def last(ny, out_in, dx_in, gw_in, out_ref, dx_ref, dw_ref, dr_ref, dw_out, dr_out, sem):
    rows = BLOCK // ny
    out_copy = pltpu.make_async_copy(out_in, out_ref, sem.at[0])
    dx_copy = pltpu.make_async_copy(dx_in, dx_ref, sem.at[1])
    dw_copy = pltpu.make_async_copy(dw_out, dw_ref, sem.at[2])
    dr_copy = pltpu.make_async_copy(dr_out, dr_ref, sem.at[3])
    out_copy.start()
    dx_copy.start()
    low = lax.broadcasted_iota(jnp.int32, (rows, LANES), 1) < 64
    for pair in range(ny // 2):
        cols = slice(pair * LANES, (pair + 1) * LANES)
        even = gw_in[2 * pair].astype(F32)
        odd = gw_in[2 * pair + 1].astype(F32)
        dw_out[:, cols] = jnp.where(low, even, pltpu.roll(odd, 64, 1)).astype(BF16)
        dr_out[:, cols] = jnp.where(low, pltpu.roll(even, 64, 1), odd).astype(BF16)
    dw_copy.start()
    dr_copy.start()
    out_copy.wait()
    dx_copy.wait()
    dw_copy.wait()
    dr_copy.wait()


def on_device(nx, nz, ny, inputs, step_sizes, decay_rates, state_write, state_read, doc_lengths, out_grad):
    rows = BLOCK // ny
    piece = STATE // (nz // PAIRS)
    vmem = pl.BlockSpec(memory_space=pltpu.VMEM)
    anywhere = pl.BlockSpec(memory_space=pl.ANY)
    wide_shape = jax.ShapeDtypeStruct(inputs.shape, BF16)
    thin_shape = jax.ShapeDtypeStruct(state_write.shape, BF16)
    bf = lambda *shape: pltpu.VMEM(shape, BF16)
    fl = lambda *shape: pltpu.VMEM(shape, F32)
    outs = pl.pallas_call(
        functools.partial(kernel, nx, nz, ny),
        out_shape=(bf(*inputs.shape), bf(*inputs.shape), bf(ny, rows, LANES)),
        in_specs=[anywhere] * 7,
        out_specs=(vmem, vmem, vmem),
        scratch_shapes=[
            bf(*step_sizes.shape), bf(*state_write.shape),
            bf(*state_read.shape), pltpu.SMEM(decay_rates.shape, F32), pltpu.SMEM((DOCS,), jnp.int32),
            bf(ny, rows, 2 * LANES), bf(ny, rows, 2 * LANES),
            bf(ny, rows, WIDE), bf(ny, rows, WIDE),
            fl(PAIRS, 1, LANES), fl(nz, 1, LANES),
            bf(nz, piece, LANES), bf(nz, piece, LANES), bf(nz, piece, LANES), bf(nz, piece, LANES),
            fl(piece + 8, LANES), fl(nx, piece + 8, LANES), fl(piece, LANES), fl(nx, piece, LANES),
            bf(nz, piece, LANES), bf(nz, piece, LANES), bf(nz, piece, LANES), bf(nz, piece, LANES),
            bf(ny, rows, WIDE), bf(ny, rows, WIDE), bf(ny, rows, LANES),
            fl(BLOCK, HEADS_HERE * LANES), fl(HEADS_HERE, BLOCK), fl(BLOCK, BLOCK), fl(BLOCK, BLOCK),
            fl(BLOCK, BLOCK), bf(BLOCK, WIDE), bf(BLOCK, WIDE), fl(BLOCK, WIDE), fl(BLOCK, WIDE),
            fl(BLOCK, WIDE), fl(BLOCK, WIDE),
            pltpu.SemaphoreType.DMA((6,)), pltpu.SemaphoreType.DMA((6,)),
            pltpu.SemaphoreType.DMA((5,)), pltpu.SemaphoreType.DMA((5,)),
            pltpu.SemaphoreType.DMA((2,)), pltpu.SemaphoreType.DMA((2,)),
            pltpu.SemaphoreType.DMA((7,)), pltpu.SemaphoreType.REGULAR((4,)),
        ],
        compiler_params=pltpu.CompilerParams(collective_id=0, has_side_effects=True),
    )(inputs, step_sizes, decay_rates, state_write, state_read, doc_lengths, out_grad)
    return pl.pallas_call(
        functools.partial(last, ny),
        out_shape=(wide_shape, wide_shape, thin_shape, thin_shape),
        in_specs=[vmem, vmem, vmem],
        out_specs=(anywhere, anywhere, anywhere, anywhere),
        scratch_shapes=[bf(*state_write.shape), bf(*state_read.shape), pltpu.SemaphoreType.DMA((4,))],
    )(*[pltpu.with_memory_space_constraint(part, pltpu.VMEM) for part in outs])


def solution(mesh):
    nctx, ny = mesh.shape["ctx"], mesh.shape["head"]
    nz = 16 if nctx % 16 == 0 else nctx // 2
    nx = nctx // nz
    rows = P(("ctx", "head"), None)
    return jax.shard_map(
        functools.partial(on_device, nx, nz, ny),
        mesh=mesh,
        in_specs=(rows, rows, P("head"), rows, rows, P(), rows),
        out_specs=(rows, rows, rows, rows),
        check_vma=False,
    )
```

```python
import functools

import jax
import jax.numpy as jnp
from jax import lax
from jax.experimental import pallas as pl
from jax.experimental.pallas import tpu as pltpu
from jax.sharding import PartitionSpec as P

HEAD_DIM = 64
STATE = 64
BLOCK = 256
DOCS = 16
HEADS_HERE = 8
WIDE = HEADS_HERE * HEAD_DIM
PAIRS = HEADS_HERE // 2
LANES = 128
NEG = -1e30
F32 = jnp.float32
BF16 = jnp.bfloat16


def dot_nn(a, b):
    return lax.dot_general(a, b, (((1,), (0,)), ((), ())), preferred_element_type=F32)


def dot_nt(a, b):
    return lax.dot_general(a, b, (((1,), (1,)), ((), ())), preferred_element_type=F32)


def dot_tn(a, b):
    return lax.dot_general(a, b, (((0,), (0,)), ((), ())), preferred_element_type=F32)


def kernel(
    nx, nz, ny,
    x_ref, step_ref, rate_ref, w_ref, r_ref, doc_ref, g_ref,
    out_ref, dx_ref, gw_recv,
    step_in, w_in, r_in, rate_in, doc_in,
    sw_send, sw_buf, v_buf, g_buf,
    dec_send, dec_recv, f_send, f_recv, b_send, b_recv,
    xf_send, xf_recv, xb_send, xb_recv,
    rf_send, rf_recv, rb_send, rb_recv,
    out_send, dx_send, gw_send,
    run_col, run_row, bias_ref, score_ref, dscore_ref, ev_ref, cg_ref, loc_ref, dv_ref, fin_ref, fout_ref,
    y_ssem, y_rsem, z_ssem, z_rsem, x_ssem, x_rsem, own_sem, ready,
):
    rows = BLOCK // ny
    blocks_of = nz // PAIRS
    piece = STATE // blocks_of
    ctx = lax.axis_index("ctx")
    me = lax.axis_index("head")
    zme = lax.rem(ctx, nz)
    xme = lax.div(ctx, nz)
    base = xme * nz

    def y_peer(k):
        return lax.rem(me + k, ny)

    def z_peer(k):
        return lax.rem(zme + k, nz)

    def x_peer(k):
        return lax.rem(xme + k, nx)

    def y_copy(cat, k, src, dst):
        return pltpu.make_async_remote_copy(
            src_ref=src, dst_ref=dst, send_sem=y_ssem.at[cat], recv_sem=y_rsem.at[cat],
            device_id={"ctx": ctx, "head": y_peer(k)}, device_id_type=pl.DeviceIdType.MESH)

    def z_copy(cat, k, src, dst):
        return pltpu.make_async_remote_copy(
            src_ref=src, dst_ref=dst, send_sem=z_ssem.at[cat], recv_sem=z_rsem.at[cat],
            device_id={"ctx": base + z_peer(k), "head": me}, device_id_type=pl.DeviceIdType.MESH)

    def x_copy(cat, k, src, dst):
        return pltpu.make_async_remote_copy(
            src_ref=src, dst_ref=dst, send_sem=x_ssem.at[cat], recv_sem=x_rsem.at[cat],
            device_id={"ctx": x_peer(k) * nz + zme, "head": me}, device_id_type=pl.DeviceIdType.MESH)

    def signal_y(sem, k):
        pl.semaphore_signal(
            sem, inc=1, device_id={"ctx": ctx, "head": y_peer(k)}, device_id_type=pl.DeviceIdType.MESH)

    def signal_z(sem, k):
        pl.semaphore_signal(
            sem, inc=1, device_id={"ctx": base + z_peer(k), "head": me}, device_id_type=pl.DeviceIdType.MESH)

    def signal_x(sem, k):
        pl.semaphore_signal(
            sem, inc=1, device_id={"ctx": x_peer(k) * nz + zme, "head": me}, device_id_type=pl.DeviceIdType.MESH)

    def wide(at):
        return pl.ds(pl.multiple_of(at * WIDE, WIDE), WIDE)

    def far_first(n):
        return sorted(range(1, n), key=lambda k: (-min(k, n - k), k))

    def near_first(n):
        return far_first(n)[::-1]

    def some(ref, n):
        return ref.at[pl.ds(0, n - 1)]

    def some_wide(ref):
        return ref.at[:, pl.ds(0, (ny - 1) * WIDE)]

    barrier = pltpu.get_barrier_semaphore()
    x_near = sorted({1, nx - 1})
    for k in far_first(ny):
        signal_y(barrier, k)
    for k in x_near:
        signal_x(barrier, k)
    for k in (1, nz - 1):
        signal_z(barrier, k)

    fetch = [
        pltpu.make_async_copy(src, dst, own_sem.at[i])
        for i, (src, dst) in enumerate((
            (step_ref, step_in), (w_ref, w_in), (r_ref, r_in), (x_ref.at[:, wide(me)], v_buf.at[me]),
            (g_ref.at[:, wide(me)], g_buf.at[me]),
            (doc_ref, doc_in), (rate_ref, rate_in)))
    ]
    for copy in fetch:
        copy.start()

    low = lax.broadcasted_iota(jnp.int32, (rows, LANES), 1) < 64
    for copy in fetch[0:3]:
        copy.wait()
    steps_here = step_in[...]
    if ny * HEADS_HERE < LANES:
        steps_here = jnp.concatenate([steps_here, jnp.zeros((rows, LANES - ny * HEADS_HERE), BF16)], axis=1)
    for pair in range(ny // 2):
        cols = slice(pair * LANES, (pair + 1) * LANES)
        w2 = w_in[:, cols].astype(F32)
        r2 = r_in[:, cols].astype(F32)
        sw_send[2 * pair, :, 0:LANES] = steps_here
        sw_send[2 * pair + 1, :, 0:LANES] = steps_here
        sw_send[2 * pair, :, LANES:2 * LANES] = jnp.where(low, w2, pltpu.roll(r2, 64, 1)).astype(BF16)
        sw_send[2 * pair + 1, :, LANES:2 * LANES] = jnp.where(low, pltpu.roll(w2, 64, 1), r2).astype(BF16)
    pl.semaphore_wait(barrier, ny - 1 + len(x_near) + 2)

    steps_z = []
    radius = 1
    while radius < nz // 2:
        steps_z.append(radius)
        radius *= 2

    def reach_start(at):
        if at < len(steps_z):
            for k in (steps_z[at], nz - steps_z[at]):
                signal_z(ready.at[at], k)

    def reach_end(at):
        if at < len(steps_z):
            pl.semaphore_wait(ready.at[at], 2)

    reach_start(0)
    if nx > 2:
        signal_x(ready.at[3], 1)
        signal_x(ready.at[3], nx - 1)

    for k in near_first(ny):
        y_copy(0, k, sw_send.at[y_peer(k)], sw_buf.at[me]).start()
    for k in near_first(ny):
        y_copy(1, k, x_ref.at[:, wide(y_peer(k))], v_buf.at[me]).start()
    reach_end(0)
    reach_start(1)
    for k in near_first(ny):
        y_copy(2, k, g_ref.at[:, wide(y_peer(k))], g_buf.at[me]).start()

    fetch[5].wait()
    fetch[6].wait()
    first = ctx * BLOCK
    starts, at = [], jnp.int32(0)
    for k in range(DOCS):
        starts.append(at)
        at = at + doc_in[k]

    def segment(pos):
        seg = jnp.where(starts[0] <= pos, 1, 0)
        for k in range(1, DOCS):
            seg = seg + jnp.where(starts[k] <= pos, 1, 0)
        return seg

    seg_before = segment(first - 1)
    seg_last = segment(first + BLOCK - 1)
    seg_col = segment(first + lax.broadcasted_iota(jnp.int32, (BLOCK, LANES), 0))
    seg_row = segment(first + lax.broadcasted_iota(jnp.int32, (8, BLOCK), 1))[0:1]
    if nx > 2:
        pl.semaphore_wait(ready.at[3], 2)
    reach_end(1)
    reach_start(2)
    fetch[3].wait()
    fetch[4].wait()
    sw_buf[me] = sw_send[me]
    row_i = lax.broadcasted_iota(jnp.int32, (BLOCK, BLOCK), 0)
    col_i = lax.broadcasted_iota(jnp.int32, (BLOCK, BLOCK), 1)
    causal = row_i >= col_i
    seg_wide = jnp.concatenate([seg_col, seg_col], axis=1)
    bias_ref[...] = jnp.where(causal & (seg_wide == seg_row), 0.0, NEG)
    dscore_ref[...] = jnp.zeros((BLOCK, BLOCK), F32)
    through = jnp.where(seg_last == seg_before, 1.0, 0.0)

    y_copy(0, 1, some(sw_send, ny), some(sw_buf, ny)).wait_recv()
    steps = sw_buf[:, :, 0:LANES].reshape(BLOCK, LANES)
    wr = sw_buf[:, :, LANES:2 * LANES].reshape(BLOCK, LANES)
    pick = (lax.broadcasted_iota(jnp.int32, (LANES, HEADS_HERE * LANES), 0) == me * HEADS_HERE
            + lax.broadcasted_iota(jnp.int32, (LANES, HEADS_HERE * LANES), 1) // LANES)
    spread_steps = dot_nn(steps, jnp.where(pick, 1.0, 0.0).astype(BF16)).astype(BF16)
    summed = dot_nn(jnp.where(causal, 1.0, 0.0).astype(BF16), spread_steps)
    pick_row = (lax.broadcasted_iota(jnp.int32, (16, LANES), 1) == me * HEADS_HERE
                + lax.broadcasted_iota(jnp.int32, (16, LANES), 0))
    steps_row = dot_nt(jnp.where(pick_row, 1.0, 0.0).astype(BF16), steps).astype(BF16)
    summed_row = dot_nn(steps_row, jnp.where(row_i <= col_i, 1.0, 0.0).astype(BF16))
    for h in range(HEADS_HERE):
        run_col[:, h * LANES:(h + 1) * LANES] = summed[:, h * LANES:(h + 1) * LANES] * (-rate_in[h])
        run_row[h:h + 1, :] = summed_row[h:h + 1, :] * (-rate_in[h])
    low = lax.broadcasted_iota(jnp.int32, (BLOCK, LANES), 1) < 64
    low_row = low[0:1]

    def pair_run(t):
        return jnp.where(low, run_col[:, 2 * t * LANES:(2 * t + 1) * LANES],
                         run_col[:, (2 * t + 1) * LANES:(2 * t + 2) * LANES])

    def pair_last(t):
        return jnp.where(low_row, run_col[BLOCK - 1:BLOCK, 2 * t * LANES:(2 * t + 1) * LANES],
                         run_col[BLOCK - 1:BLOCK, (2 * t + 1) * LANES:(2 * t + 2) * LANES])

    def factor_in(t):
        return jnp.where(seg_col == seg_before, jnp.exp(pair_run(t)), 0.0)

    def factor_out(t):
        return jnp.where(seg_col == seg_last, jnp.exp(pair_last(t) - pair_run(t)), 0.0)

    for t in range(PAIRS):
        dec_send[t] = jnp.exp(pair_last(t)) * through
    dec_recv[zme] = dec_send[zme // blocks_of]

    for t in range(PAIRS):
        cols = slice(t * LANES, (t + 1) * LANES)
        fout_ref[:, cols] = factor_out(t)
        fin_ref[:, cols] = factor_in(t)
    rw = pltpu.roll(wr.astype(F32), 64, 1)
    writers = wr[:, 0:64]
    readers = rw[:, 0:64].astype(BF16)
    read_low = jnp.where(low, rw, 0.0).astype(BF16)
    write_high = jnp.where(low, 0.0, rw).astype(BF16)
    score_ref[...] = dot_nt(readers, writers)
    turned = jnp.transpose(wr.astype(F32)).astype(BF16)

    reach_end(2)
    for k in far_first(nz):
        z_copy(0, k, dec_send.at[lax.div(z_peer(k), blocks_of)], dec_recv.at[zme]).start()

    y_copy(1, 1, some_wide(x_ref), some(v_buf, ny)).wait_recv()
    for t in range(PAIRS):
        cols = slice(t * LANES, (t + 1) * LANES)
        values = v_buf[:, :, cols].reshape(BLOCK, LANES)
        ev = (values.astype(F32) * fout_ref[:, cols]).astype(BF16)
        ev_ref[:, cols] = ev
        added = dot_nn(turned[0:STATE], ev).astype(BF16)
        f_send[t * blocks_of:(t + 1) * blocks_of] = added.reshape(blocks_of, piece, LANES)
    for k in far_first(nz):
        z_copy(1, k, f_send.at[z_peer(k)], f_recv.at[zme]).start()
    f_recv[zme] = f_send[zme]

    y_copy(2, 1, some_wide(g_ref), some(g_buf, ny)).wait_recv()
    for t in range(PAIRS):
        cols = slice(t * LANES, (t + 1) * LANES)
        grads = g_buf[:, :, cols].reshape(BLOCK, LANES)
        cg = (grads.astype(F32) * fin_ref[:, cols]).astype(BF16)
        cg_ref[:, cols] = cg
        added = dot_nn(turned[STATE:2 * STATE], cg).astype(BF16)
        b_send[t * blocks_of:(t + 1) * blocks_of] = added.reshape(blocks_of, piece, LANES)
    for k in far_first(nz):
        z_copy(2, k, b_send.at[z_peer(k)], b_recv.at[zme]).start()
    b_recv[zme] = b_send[zme]

    low_one = jnp.where(low_row, 1.0, 0.0).astype(BF16)
    high_one = jnp.where(low_row, 0.0, 1.0).astype(BF16)

    def inside(t, carry):
        cols = pl.ds(pl.multiple_of(t * LANES, LANES), LANES)
        values = v_buf[:, :, cols].reshape(BLOCK, LANES)
        grads = g_buf[:, :, cols].reshape(BLOCK, LANES)
        local = jnp.zeros((BLOCK, LANES), F32)
        dvalue = jnp.zeros((BLOCK, LANES), F32)
        for half, ones in ((0, low_one), (1, high_one)):
            h = 2 * t + half
            column = run_col[:, pl.ds(pl.multiple_of(h * LANES, LANES), LANES)]
            row = run_row[pl.ds(h, 1), :]
            factor = jnp.exp(jnp.concatenate([column, column], axis=1) - row + bias_ref[...])
            weights = (score_ref[...] * factor).astype(BF16)
            half_grads = grads * ones
            local = local + dot_nn(weights, values * ones)
            dscore_ref[...] += dot_nt(half_grads, values) * factor
            dvalue = dvalue + dot_tn(weights, half_grads)
        loc_ref[:, cols] = local
        dv_ref[:, cols] = dvalue
        return carry

    lax.fori_loop(0, 4, inside, 0)

    z_copy(0, 1, some(dec_recv, nz), some(dec_recv, nz)).wait_recv()
    z_copy(1, 1, some(f_send, nz), some(f_recv, nz)).wait_recv()
    total = jnp.zeros((piece, LANES), F32)
    product = jnp.ones((1, LANES), F32)
    for z in range(nz):
        total = dec_recv[z] * total + f_recv[z].astype(F32)
        product = dec_recv[z] * product
    xf_send[0:piece] = total
    xf_send[piece:piece + 8] = jnp.broadcast_to(product, (8, LANES))
    for k in far_first(nx):
        x_copy(0, k, xf_send, xf_recv.at[xme]).start()
    xf_recv[xme] = xf_send[...]
    z_copy(2, 1, some(b_send, nz), some(b_recv, nz)).wait_recv()
    total = jnp.zeros((piece, LANES), F32)
    for z in reversed(range(nz)):
        total = dec_recv[z] * total + b_recv[z].astype(F32)
    xb_send[...] = total
    for k in far_first(nx):
        x_copy(1, k, xb_send, xb_recv.at[xme]).start()
    xb_recv[xme] = xb_send[...]


    x_copy(0, 1, some(xf_recv, nx), some(xf_recv, nx)).wait_recv()
    state = jnp.zeros((piece, LANES), F32)
    for x in range(nx):
        longer = xf_recv[x, piece:piece + 1] * state + xf_recv[x, 0:piece]
        state = jnp.where(x < xme, longer, state)
    for z in range(nz):
        rf_send[z] = state.astype(BF16)
        state = dec_recv[z] * state + f_recv[z].astype(F32)
    for k in far_first(nz):
        z_copy(3, k, rf_send.at[z_peer(k)], rf_recv.at[zme]).start()
    rf_recv[zme] = rf_send[zme]

    x_copy(1, 1, some(xb_recv, nx), some(xb_recv, nx)).wait_recv()
    state = jnp.zeros((piece, LANES), F32)
    for x in reversed(range(nx)):
        longer = xf_recv[x, piece:piece + 1] * state + xb_recv[x]
        state = jnp.where(x > xme, longer, state)
    for z in reversed(range(nz)):
        rb_send[z] = state.astype(BF16)
        state = dec_recv[z] * state + b_recv[z].astype(F32)
    for k in far_first(nz):
        z_copy(4, k, rb_send.at[z_peer(k)], rb_recv.at[zme]).start()
    rb_recv[zme] = rb_send[zme]

    dscore = dscore_ref[...].astype(BF16)
    gw = dot_nn(dscore, write_high) + dot_tn(dscore, read_low)
    nothing = jnp.zeros((STATE, LANES), BF16)

    z_copy(3, 1, some(rf_send, nz), some(rf_recv, nz)).wait_recv()
    for t in range(PAIRS):
        cols = slice(t * LANES, (t + 1) * LANES)
        entering = rf_recv[t * blocks_of:(t + 1) * blocks_of].reshape(STATE, LANES)
        result = loc_ref[:, cols] + fin_ref[:, cols] * dot_nn(readers, entering)
        out_send[:, :, cols] = result.astype(BF16).reshape(ny, rows, LANES)
    for k in far_first(ny):
        y_copy(3, k, out_send.at[y_peer(k)], out_ref.at[:, wide(me)]).start()
    out_ref[:, wide(me)] = out_send[me]
    for t in range(PAIRS):
        cols = slice(t * LANES, (t + 1) * LANES)
        entering = rf_recv[t * blocks_of:(t + 1) * blocks_of].reshape(STATE, LANES)
        gw = gw + dot_nt(cg_ref[:, cols], jnp.concatenate([nothing, entering], axis=0))

    z_copy(4, 1, some(rb_send, nz), some(rb_recv, nz)).wait_recv()
    for t in range(PAIRS):
        cols = slice(t * LANES, (t + 1) * LANES)
        leaving = rb_recv[t * blocks_of:(t + 1) * blocks_of].reshape(STATE, LANES)
        result = dv_ref[:, cols] + fout_ref[:, cols] * dot_nn(writers, leaving)
        dx_send[:, :, cols] = result.astype(BF16).reshape(ny, rows, LANES)
    for k in far_first(ny):
        y_copy(4, k, dx_send.at[y_peer(k)], dx_ref.at[:, wide(me)]).start()
    dx_ref[:, wide(me)] = dx_send[me]
    for t in range(PAIRS):
        cols = slice(t * LANES, (t + 1) * LANES)
        leaving = rb_recv[t * blocks_of:(t + 1) * blocks_of].reshape(STATE, LANES)
        gw = gw + dot_nt(ev_ref[:, cols], jnp.concatenate([leaving, nothing], axis=0))
    gw_send[...] = gw.astype(BF16).reshape(ny, rows, LANES)
    for k in far_first(ny):
        y_copy(5, k, gw_send.at[y_peer(k)], gw_recv.at[me]).start()
    gw_recv[me] = gw_send[me]

    y_copy(0, 1, some(sw_send, ny), some(sw_buf, ny)).wait_send()
    y_copy(1, 1, some_wide(x_ref), some(v_buf, ny)).wait_send()
    y_copy(2, 1, some_wide(g_ref), some(g_buf, ny)).wait_send()
    z_copy(0, 1, some(dec_recv, nz), some(dec_recv, nz)).wait_send()
    z_copy(1, 1, some(f_send, nz), some(f_recv, nz)).wait_send()
    z_copy(2, 1, some(b_send, nz), some(b_recv, nz)).wait_send()
    z_copy(3, 1, some(rf_send, nz), some(rf_recv, nz)).wait_send()
    z_copy(4, 1, some(rb_send, nz), some(rb_recv, nz)).wait_send()
    x_copy(0, 1, some(xf_recv, nx), some(xf_recv, nx)).wait_send()
    x_copy(1, 1, some(xb_recv, nx), some(xb_recv, nx)).wait_send()
    y_copy(3, 1, some(out_send, ny), some_wide(out_ref)).wait()
    y_copy(4, 1, some(dx_send, ny), some_wide(dx_ref)).wait()
    y_copy(5, 1, some(gw_send, ny), some(gw_recv, ny)).wait()


def last(ny, out_in, dx_in, gw_in, out_ref, dx_ref, dw_ref, dr_ref, dw_out, dr_out, sem):
    rows = BLOCK // ny
    out_copy = pltpu.make_async_copy(out_in, out_ref, sem.at[0])
    dx_copy = pltpu.make_async_copy(dx_in, dx_ref, sem.at[1])
    dw_copy = pltpu.make_async_copy(dw_out, dw_ref, sem.at[2])
    dr_copy = pltpu.make_async_copy(dr_out, dr_ref, sem.at[3])
    out_copy.start()
    dx_copy.start()
    low = lax.broadcasted_iota(jnp.int32, (rows, LANES), 1) < 64
    for pair in range(ny // 2):
        cols = slice(pair * LANES, (pair + 1) * LANES)
        even = gw_in[2 * pair].astype(F32)
        odd = gw_in[2 * pair + 1].astype(F32)
        dw_out[:, cols] = jnp.where(low, even, pltpu.roll(odd, 64, 1)).astype(BF16)
        dr_out[:, cols] = jnp.where(low, pltpu.roll(even, 64, 1), odd).astype(BF16)
    dw_copy.start()
    dr_copy.start()
    out_copy.wait()
    dx_copy.wait()
    dw_copy.wait()
    dr_copy.wait()


def on_device(nx, nz, ny, inputs, step_sizes, decay_rates, state_write, state_read, doc_lengths, out_grad):
    rows = BLOCK // ny
    piece = STATE // (nz // PAIRS)
    vmem = pl.BlockSpec(memory_space=pltpu.VMEM)
    anywhere = pl.BlockSpec(memory_space=pl.ANY)
    wide_shape = jax.ShapeDtypeStruct(inputs.shape, BF16)
    thin_shape = jax.ShapeDtypeStruct(state_write.shape, BF16)
    bf = lambda *shape: pltpu.VMEM(shape, BF16)
    fl = lambda *shape: pltpu.VMEM(shape, F32)
    outs = pl.pallas_call(
        functools.partial(kernel, nx, nz, ny),
        out_shape=(bf(*inputs.shape), bf(*inputs.shape), bf(ny, rows, LANES)),
        in_specs=[anywhere] * 7,
        out_specs=(vmem, vmem, vmem),
        scratch_shapes=[
            bf(*step_sizes.shape), bf(*state_write.shape),
            bf(*state_read.shape), pltpu.SMEM(decay_rates.shape, F32), pltpu.SMEM((DOCS,), jnp.int32),
            bf(ny, rows, 2 * LANES), bf(ny, rows, 2 * LANES),
            bf(ny, rows, WIDE), bf(ny, rows, WIDE),
            fl(PAIRS, 1, LANES), fl(nz, 1, LANES),
            bf(nz, piece, LANES), bf(nz, piece, LANES), bf(nz, piece, LANES), bf(nz, piece, LANES),
            fl(piece + 8, LANES), fl(nx, piece + 8, LANES), fl(piece, LANES), fl(nx, piece, LANES),
            bf(nz, piece, LANES), bf(nz, piece, LANES), bf(nz, piece, LANES), bf(nz, piece, LANES),
            bf(ny, rows, WIDE), bf(ny, rows, WIDE), bf(ny, rows, LANES),
            fl(BLOCK, HEADS_HERE * LANES), fl(HEADS_HERE, BLOCK), fl(BLOCK, BLOCK), fl(BLOCK, BLOCK),
            fl(BLOCK, BLOCK), bf(BLOCK, WIDE), bf(BLOCK, WIDE), fl(BLOCK, WIDE), fl(BLOCK, WIDE),
            fl(BLOCK, WIDE), fl(BLOCK, WIDE),
            pltpu.SemaphoreType.DMA((6,)), pltpu.SemaphoreType.DMA((6,)),
            pltpu.SemaphoreType.DMA((5,)), pltpu.SemaphoreType.DMA((5,)),
            pltpu.SemaphoreType.DMA((2,)), pltpu.SemaphoreType.DMA((2,)),
            pltpu.SemaphoreType.DMA((7,)), pltpu.SemaphoreType.REGULAR((4,)),
        ],
        compiler_params=pltpu.CompilerParams(collective_id=0, has_side_effects=True),
    )(inputs, step_sizes, decay_rates, state_write, state_read, doc_lengths, out_grad)
    return pl.pallas_call(
        functools.partial(last, ny),
        out_shape=(wide_shape, wide_shape, thin_shape, thin_shape),
        in_specs=[vmem, vmem, vmem],
        out_specs=(anywhere, anywhere, anywhere, anywhere),
        scratch_shapes=[bf(*state_write.shape), bf(*state_read.shape), pltpu.SemaphoreType.DMA((4,))],
    )(*[pltpu.with_memory_space_constraint(part, pltpu.VMEM) for part in outs])


def solution(mesh):
    nctx, ny = mesh.shape["ctx"], mesh.shape["head"]
    nz = 16 if nctx % 16 == 0 else nctx // 2
    nx = nctx // nz
    rows = P(("ctx", "head"), None)
    return jax.shard_map(
        functools.partial(on_device, nx, nz, ny),
        mesh=mesh,
        in_specs=(rows, rows, P("head"), rows, rows, P(), rows),
        out_specs=(rows, rows, rows, rows),
        check_vma=False,
    )
```
